512 devices in a mesh: ctx: 64 (over y, x, core), head: 8 (over z).
Axes of the slice: x: 4, y: 8, z: 8, core: 2. Of those that a mesh axis runs over, the one named last changes fastest.
Arguments:
- head_input: bfloat16 [32768, 5120], P('ctx', 'head'), may hold values from -6 to 6
- bc_input: bfloat16 [32768, 256], P('ctx'), may hold values from -3 to 3
- conv_x: float32 [4, 5120], P(None, 'head'), may hold values from -3 to 3
- conv_bc: float32 [4, 256], replicated, may hold values from -3 to 3
- log_decay: float32 [80, 32768], P('head', 'ctx'), may hold values from -2 to 0
- d_skip: float32 [80], P('head'), may hold values from 0.5 to 2
- gate_z: bfloat16 [32768, 5120], P('ctx', 'head'), may hold values from -400 to 400
- norm_gain: float32 [5120], P('head'), may hold values from 0.1 to 1.9
- w_out: bfloat16 [5120, 2560], P('head'), may hold values from -0.078125 to 0.078125
Outputs:
- layer_out: bfloat16 [32768, 2560], P('ctx', 'head')
The draws below stay inside these ranges and needn't reach their ends.
All inputs are finite; a program needn't handle non-finite values.
Results may differ from the reference program's by a relative error of at most 0.013.
Values may be sent and summed in bfloat16 or wider, within the bound.
A program may use at most 64 MiB of HBM per device.

```python
import jax
import jax.numpy as jnp
from jax import lax

D = 2560
H = 80
P_SIZE = 64
N = 128
K = 4
TOK_DEV = 512
DI = 5120
HEAD_DEV = 10
GENOME_LENGTH = 32768
N_CTX = 64


def draw_log_decay(key, part):
    generator_seeds = jax.random.split(key, 7)
    head_order = jax.random.permutation(generator_seeds[0], H)
    slow_count = H // 2
    slow_heads = head_order < slow_count
    slow_rate = jnp.exp(jax.random.uniform(generator_seeds[1], (H,), jnp.float32, jnp.log(0.05 / GENOME_LENGTH), jnp.log(0.5 / GENOME_LENGTH)))
    fast_rate = jnp.exp(jax.random.uniform(generator_seeds[2], (H,), jnp.float32, jnp.log(0.015), jnp.log(0.04)))
    forgetting_rate = jnp.where(slow_heads, slow_rate, fast_rate)
    noise_perturbation = jnp.exp(jax.random.uniform(generator_seeds[3], (H, GENOME_LENGTH), jnp.float32, jnp.log(0.5), jnp.log(2.0)))
    piece_multiplier = jnp.exp(jax.random.uniform(generator_seeds[4], (GENOME_LENGTH // TOK_DEV,), jnp.float32, jnp.log(0.5), jnp.log(2.0)))
    piece_multiplier = jnp.repeat(piece_multiplier, TOK_DEV)
    spike_center = jax.random.randint(generator_seeds[5], (3,), 0, GENOME_LENGTH)
    spike_width_draw = jnp.log(jax.random.uniform(generator_seeds[6], (3,), jnp.float32, 0.62, 0.8))
    residue_indices = jnp.arange(GENOME_LENGTH)
    spike_log_height = jnp.sum(jnp.where(residue_indices[None, :] == spike_center[:, None], spike_width_draw[:, None], 0.0), axis=0)
    element_numbers = -forgetting_rate[:, None] * noise_perturbation * piece_multiplier[None, :] + spike_log_height[None, :]
    return element_numbers.astype(jnp.float32)


def draw_gate_z(key, part):
    generator_seeds = jax.random.split(key, 3)
    base = jax.random.truncated_normal(generator_seeds[0], -4.0, 4.0, (GENOME_LENGTH, DI), jnp.float32)
    column = jnp.arange(DI).astype(jnp.float32) / DI
    column_noise = jax.random.uniform(generator_seeds[1], (DI,), jnp.float32)
    row_noise = jax.random.uniform(generator_seeds[2], (GENOME_LENGTH,), jnp.float32)
    column_scale = jnp.exp(jnp.log(10.0) * (0.5 * column + 0.5 * column_noise))
    row_scale = jnp.exp(jnp.log(10.0) * row_noise)
    return (base * row_scale[:, None] * column_scale[None, :]).astype(jnp.bfloat16)


def steps_of(key, dims, pieces, smallest, largest):
    loudness = 1.0
    for dim, shards_of in pieces:
        steps = jax.random.uniform(jax.random.fold_in(jax.random.fold_in(key, 6), dim), (shards_of,), jnp.float32, smallest / len(pieces), largest / len(pieces))
        loudness = loudness * jnp.repeat(jnp.exp(steps), dims[dim] // shards_of).reshape((-1,) + (1,) * (len(dims) - 1 - dim))
    return loudness


def bell_draw(own_key, extent, scale, reach, cuts=(), held_as=jnp.bfloat16):
    values = scale * jax.random.normal(own_key, extent, jnp.float32)
    if cuts:
        values = values * steps_of(own_key, extent, cuts, -0.22, 0.18)
    return jnp.clip(values, -reach, reach).astype(held_as)


def setup_inputs(seed: int = 0) -> dict:
    seeds = jax.random.split(jax.random.key(seed), 10)
    head_input = bell_draw(seeds[0], (GENOME_LENGTH, DI), 1.0, 6.0, ((0, 64), (1, 8)))
    bc_input = bell_draw(seeds[1], (GENOME_LENGTH, 2 * N), 0.5, 3.0, ((0, 64),))
    conv_x = bell_draw(seeds[2], (K, DI), K ** -0.5, 3.0, ((1, 8),), jnp.float32)
    conv_bc = bell_draw(seeds[3], (K, 2 * N), K ** -0.5, 3.0, (), jnp.float32)
    log_decay = draw_log_decay(jax.random.fold_in(seeds[9], 71), 0)
    d_skip = jnp.clip(0.5 + 1.5 * jax.random.uniform(seeds[5], (H,), jnp.float32) ** steps_of(seeds[5], (H,), ((0, 8),), -0.2, 0.2), 0.5, 2.0)
    gate_z = draw_gate_z(jax.random.fold_in(seeds[9], 71), 0)
    norm_gain = jnp.clip(1.0 + 0.18 * jax.random.normal(seeds[7], (DI,), jnp.float32), 0.1, 1.9)
    w_out = bell_draw(seeds[8], (DI, D), DI ** -0.5, 0.078125, ((0, 8),))
    return {"head_input": head_input, "bc_input": bc_input, "conv_x": conv_x, "conv_bc": conv_bc, "log_decay": log_decay, "d_skip": d_skip, "gate_z": gate_z, "norm_gain": norm_gain, "w_out": w_out}


def causal_conv(signal, kernel):
    length = signal.shape[0]
    padded = jnp.concatenate([jnp.zeros((K - 1, signal.shape[1]), jnp.float32), signal.astype(jnp.float32)], axis=0)
    summed = jnp.zeros((length, signal.shape[1]), jnp.float32)
    for tap_index in range(K):
        summed = summed + kernel[tap_index] * padded[tap_index:tap_index + length]
    return summed

def block_terms(head_block, write_block, read_block, logs, incoming, skipping):
    length = logs.shape[1]
    cumulative = jnp.cumsum(logs, axis=1)
    gram_matrix = jnp.dot(read_block, write_block.T, preferred_element_type=jnp.float32)
    position = jnp.arange(length)
    lower_mask = position[:, None] >= position[None, :]
    spread = jnp.minimum(cumulative[:, :, None] - cumulative[:, None, :], 0.0)
    mixing = jnp.where(lower_mask[None], gram_matrix[None] * jnp.exp(spread), 0.0).astype(jnp.bfloat16)
    head_float = head_block.astype(jnp.float32)
    y_local = jnp.einsum('hts,shp->thp', mixing.astype(jnp.float32), head_float)
    weights = jnp.exp(cumulative[:, -1:] - cumulative)
    scaled = (head_float * weights.T[:, :, None]).astype(jnp.bfloat16)
    block_state = jnp.einsum('shp,sn->hpn', scaled.astype(jnp.float32), write_block.astype(jnp.float32))
    y_state = jnp.einsum('tn,hpn->thp', read_block.astype(jnp.float32), incoming, precision=lax.Precision.HIGHEST) * jnp.exp(cumulative).T[:, :, None]
    result = y_local + y_state + skipping[None, :, None] * head_float
    outgoing = jnp.exp(cumulative[:, -1])[:, None, None] * incoming + block_state
    return (result, outgoing)

def reference(head_input, bc_input, conv_x, conv_bc, log_decay, d_skip, gate_z, norm_gain, w_out):
    xconv = jax.nn.silu(causal_conv(head_input, conv_x)).astype(jnp.bfloat16)
    bc_conv = jax.nn.silu(causal_conv(bc_input, conv_bc)).astype(jnp.bfloat16)
    head_blocks = xconv.reshape(N_CTX, TOK_DEV, H, P_SIZE)
    write_blocks = bc_conv[:, :N].reshape(N_CTX, TOK_DEV, N)
    read_blocks = bc_conv[:, N:].reshape(N_CTX, TOK_DEV, N)
    log_blocks = log_decay.reshape(H, N_CTX, TOK_DEV).transpose(1, 0, 2)

    def advance(carried, inputs):
        head_block, write_block, read_block, logs = inputs
        result, outgoing = block_terms(head_block, write_block, read_block, logs, carried, d_skip)
        return (outgoing, result)
    _, outputs = lax.scan(advance, jnp.zeros((H, P_SIZE, N), jnp.float32), (head_blocks, write_blocks, read_blocks, log_blocks))
    ssm_out = outputs.reshape(GENOME_LENGTH, H * P_SIZE)
    gated = ssm_out * jax.nn.silu(gate_z.astype(jnp.float32))
    mean_square = lax.optimization_barrier(jnp.sum(gated * gated, axis=1)) / (H * P_SIZE)
    normed = (gated * lax.rsqrt(mean_square + 1e-05)[:, None] * norm_gain[None, :]).astype(jnp.bfloat16)
    group_width = HEAD_DEV * P_SIZE
    summed = jnp.zeros((GENOME_LENGTH, D), jnp.float32)
    for group_index in range(H // HEAD_DEV):
        lower_edge = group_index * group_width
        partial_value = jnp.dot(normed[:, lower_edge:lower_edge + group_width], w_out[lower_edge:lower_edge + group_width], preferred_element_type=jnp.float32)
        summed = summed + lax.optimization_barrier(partial_value.astype(jnp.bfloat16)).astype(jnp.float32)
    return summed.astype(jnp.bfloat16)
```

```python
import functools

import jax
import jax.numpy as jnp
from jax import lax
from jax.experimental import pallas as pl
from jax.experimental.pallas import tpu as pltpu
from jax.sharding import Mesh
from jax.sharding import PartitionSpec as P

F32 = jnp.float32
BF16 = jnp.bfloat16
MESH = pl.DeviceIdType.MESH
N = 128
K = 4
LANES = 128
ROWS = 64
SUBS = 4
CTX = ("y", "x", "c")


def split_three(value):
    high = value.astype(BF16)
    rest = value - high.astype(F32)
    middle = rest.astype(BF16)
    low = (rest - middle.astype(F32)).astype(BF16)
    return high, middle, low


def silu(value):
    small = jnp.exp(-jnp.abs(value))
    return value * jnp.where(value >= 0, 1.0, small) / (1.0 + small)


def dot(a, b, dims):
    return lax.dot_general(a, b, (dims, ((), ())), preferred_element_type=F32)


def iota(shape, dim):
    return lax.broadcasted_iota(jnp.int32, shape, dim)


def remote(source, target, send_sem, recv_sem, device):
    return pltpu.make_async_remote_copy(
        src_ref=source,
        dst_ref=target,
        send_sem=send_sem,
        recv_sem=recv_sem,
        device_id=device,
        device_id_type=MESH,
    )


def kernel(
    sizes,
    x_hbm, bc_hbm, cx_hbm, cbc_hbm, ld_hbm, d_hbm, gate_hbm, gain_hbm, w_hbm,
    out_ref,
    x_in, bc_in, cx, cbc, ld, d_skip, gate, gain, w,
    load_sem,
    halo_x, halo_bc, halo_send, halo_recv,
    xf, bcf, xc, bcc, crow, cum, cum2, gram, scaled, state,
    decay_row, decay_send, decay_recv,
    total_row, total_send, total_recv,
    row_buf, row_send, row_recv, prefix,
    y_buf, y_send, y_recv,
    c_out, carried, c_send, c_recv,
    ya, yb, u, sq_part,
    sq_buf, sq_send, sq_recv,
    chunks, long_out, short_out, long_in, short_in,
    long_send, long_recv, short_send, short_recv,
    rstd,
):
    ny, nx, nc, nz = sizes
    nj = nx * nc
    y, x, c, z = (lax.axis_index(name) for name in ("y", "x", "c", "z"))
    j = x * nc + c
    flat = y * nj + j
    slab = N // nj
    heads, length = ld.shape
    width = x_in.shape[1]
    pairs = width // LANES

    loads = [
        pltpu.make_async_copy(source, target, load_sem.at[i])
        for i, (source, target) in enumerate(
            [
                (ld_hbm, ld), (x_hbm, x_in), (bc_hbm, bc_in), (cx_hbm, cx), (cbc_hbm, cbc),
                (d_hbm, d_skip), (gate_hbm, gate), (gain_hbm, gain), (w_hbm, w),
            ]
        )
    ]
    for load in loads:
        load.start()

    def member(index):
        return {"x": lax.div(index, nc), "c": lax.rem(index, nc)}

    def at(index):
        return {"y": lax.div(index, nj), **member(lax.rem(index, nj))}

    after = at(lax.rem(flat + 1, ny * nj))
    ahead = at(lax.rem(flat + ny * nj - 1, ny * nj))

    barrier = pltpu.get_barrier_semaphore()

    def greet(device):
        pl.semaphore_signal(barrier, inc=1, device_id=device, device_id_type=MESH)

    greet(after)
    greet(ahead)
    for k in range(1, ny):
        greet({"y": lax.rem(y + k, ny)})
    for k in range(1, nz):
        greet({"z": lax.rem(z + k, nz)})
    for k in range(1, nj):
        greet(member(lax.rem(j + k, nj)))

    loads[0].wait()
    padded = jnp.concatenate([ld[...], jnp.zeros((16 - heads, length), F32)], axis=0)
    upper = (iota((length, length), 0) <= iota((length, length), 1)).astype(BF16)
    three = dot(jnp.concatenate(split_three(padded), axis=0), upper, ((1,), (0,)))
    rows = three[0:16] + (three[16:32] + three[32:48])
    for h in range(heads):
        crow[h] = rows[h : h + 1]
    stacked = jnp.concatenate(split_three(rows), axis=0)
    pick = (iota((48, width), 0) & 15) == lax.shift_right_logical(iota((48, width), 1), 6)
    cum[...] = dot(stacked, pick.astype(BF16), ((0,), (0,)))
    wide = heads * LANES
    pick2 = (iota((48, wide), 0) & 15) == lax.shift_right_logical(iota((48, wide), 1), 7)
    cum2[...] = dot(stacked, pick2.astype(BF16), ((0,), (0,)))
    decay_row[j] = cum[length - 1 : length, :]

    loads[1].wait()
    loads[2].wait()
    pl.semaphore_wait(barrier, 2 + (ny - 1) + (nz - 1) + (nj - 1))

    tail = pl.ds(length - 16, 16)
    halos = [
        remote(x_in.at[tail], halo_x, halo_send.at[0], halo_recv.at[0], after),
        remote(bc_in.at[tail], halo_bc, halo_send.at[1], halo_recv.at[1], after),
    ]

    @pl.when(flat < ny * nj - 1)
    def _():
        for copy in halos:
            copy.start()

    decays = []
    for k in range(1, nj):
        other = lax.rem(j + k, nj)
        copy = remote(
            decay_row.at[j], decay_row.at[j], decay_send.at[k], decay_recv.at[j], member(other)
        )
        copy.start()
        decays.append(copy)

    loads[3].wait()
    loads[4].wait()
    xf[0:8, :] = jnp.zeros((8, width), F32)
    bcf[0:8, :] = jnp.zeros((8, 2 * N), F32)

    def widen(i, _):
        r = pl.multiple_of(i * ROWS, ROWS)
        xf[pl.ds(r + 8, ROWS), :] = x_in[pl.ds(r, ROWS), :].astype(F32)
        bcf[pl.ds(r + 8, ROWS), :] = bc_in[pl.ds(r, ROWS), :].astype(F32)
        return 0

    lax.fori_loop(0, length // ROWS, widen, 0)

    def filtered(source, taps, r):
        block = source[pl.ds(r, ROWS + 8), :]
        total = taps[K - 1 : K, :] * block[8:]
        for tap in range(K - 1):
            total = total + taps[tap : tap + 1, :] * pltpu.roll(block, K - 1 - tap, 0)[8:]
        return silu(total).astype(BF16)

    def convolve(i, _):
        r = pl.multiple_of(i * ROWS, ROWS)
        here = pl.ds(r, ROWS)
        conv = filtered(xf, cx, r)
        xc[here, :] = conv
        bcc[here, :] = filtered(bcf, cbc, r)
        weight = jnp.exp(cum[length - 1 : length, :] - cum[here, :])
        scaled[here, :] = (conv.astype(F32) * weight).astype(BF16)
        return 0

    lax.fori_loop(1, length // ROWS, convolve, 0)

    @pl.when(flat > 0)
    def _():
        for copy in halos:
            copy.wait_recv()
        xf[0:8, :] = halo_x[8:16, :].astype(F32)
        bcf[0:8, :] = halo_bc[8:16, :].astype(F32)

    convolve(0, 0)

    state[...] = dot(bcc[:, 0:N], scaled[...], ((0,), (0,))).astype(BF16)
    row_buf[j] = state[pl.ds(pl.multiple_of(j * slab, slab), slab), :]
    sent = []
    for k in range(1, nj):
        other = lax.rem(j + k, nj)
        copy = remote(
            state.at[pl.ds(pl.multiple_of(other * slab, slab), slab)],
            row_buf.at[j],
            row_send.at[k],
            row_recv.at[j],
            member(other),
        )
        copy.start()
        sent.append(copy)

    for k in range(1, nj):
        other = lax.rem(j + k, nj)
        remote(
            decay_row.at[other], decay_row.at[other], decay_send.at[k], decay_recv.at[other],
            member(other),
        ).wait_recv()
    whole = decay_row[0]
    for i in range(1, nj):
        whole = whole + decay_row[i]
    total_row[y] = whole
    totals = []
    for k in range(1, ny):
        copy = remote(
            total_row.at[y], total_row.at[y], total_send.at[k], total_recv.at[y],
            {"y": lax.rem(y + k, ny)},
        )
        copy.start()
        totals.append(copy)

    gram[...] = dot(bcc[:, N : 2 * N], bcc[:, 0:N], ((1,), (1,)))
    left = iota((LANES, LANES), 1) < 64
    causal = iota((LANES, LANES), 0) >= iota((LANES, LANES), 1)
    loads[5].wait()

    def local_pair(i, _):
        lanes = pl.ds(pl.multiple_of(i * LANES, LANES), LANES)
        for block in range(length // LANES):
            t = slice(block * LANES, (block + 1) * LANES)
            results = []
            for side in range(2):
                h = 2 * i + side
                here = cum2[t, pl.ds(pl.multiple_of(h * LANES, LANES), LANES)]
                parts = []
                for other in range(block + 1):
                    s = slice(other * LANES, (other + 1) * LANES)
                    spread = here - crow[h, :, s]
                    if other == block:
                        part = jnp.where(causal, gram[t, s] * jnp.exp(jnp.minimum(spread, 0.0)), 0.0)
                    else:
                        part = gram[t, s] * jnp.exp(spread)
                    parts.append(part.astype(BF16))
                mixing = parts[0] if block == 0 else jnp.concatenate(parts, axis=1)
                results.append(dot(mixing, xc[0 : (block + 1) * LANES, lanes], ((1,), (0,))))
            skip = jnp.where(left, d_skip[2 * i], d_skip[2 * i + 1])
            ya[t, lanes] = jnp.where(left, results[0], results[1]) + skip * xc[t, lanes].astype(F32)
        return 0

    lax.fori_loop(0, 2, local_pair, 0)

    for k in range(1, nj):
        other = lax.rem(j + k, nj)
        remote(
            row_buf.at[other], row_buf.at[other], row_send.at[k], row_recv.at[other], member(other)
        ).wait_recv()
    running = jnp.zeros((slab, width), F32)
    for i in range(nj):
        prefix[i] = running
        running = jnp.exp(decay_row[i]) * running + row_buf[i].astype(F32)
    y_buf[y] = running.astype(BF16)
    for k in range(1, ny):

        @pl.when(y + k < ny)
        def _(k=k):
            remote(
                y_buf.at[y], y_buf.at[y], y_send.at[k], y_recv.at[y], {"y": lax.rem(y + k, ny)}
            ).start()

    lax.fori_loop(2, pairs, local_pair, 0)

    loads[6].wait()

    def gates(i, _):
        here = pl.ds(pl.multiple_of(i * ROWS, ROWS), ROWS)
        factor = silu(gate[here, :].astype(F32))
        ya[here, :] = ya[here, :] * factor
        yb[here, :] = jnp.exp(cum[here, :]) * factor
        return 0

    lax.fori_loop(0, length // ROWS, gates, 0)

    for k in range(1, ny):
        other = lax.rem(y + k, ny)
        remote(
            total_row.at[other], total_row.at[other], total_send.at[k], total_recv.at[other],
            {"y": other},
        ).wait_recv()
    for k in range(1, ny):

        @pl.when(y >= k)
        def _(k=k):
            other = lax.rem(y - k + ny, ny)
            remote(
                y_buf.at[other], y_buf.at[other], y_send.at[k], y_recv.at[other], {"y": other}
            ).wait_recv()

    def earlier(i, total):
        return jnp.exp(total_row[i]) * total + y_buf[i].astype(F32)

    base = lax.fori_loop(0, y, earlier, jnp.zeros((slab, width), F32))
    fade = jnp.zeros((1, width), F32)
    for i in range(nj):
        c_out[i] = (jnp.exp(fade) * base + prefix[i]).astype(BF16)
        fade = fade + decay_row[i]
    mine = pl.ds(pl.multiple_of(j * slab, slab), slab)
    carried[mine, :] = c_out[j]
    returned = []
    for k in range(1, nj):
        other = lax.rem(j + k, nj)
        copy = remote(c_out.at[other], carried.at[mine], c_send.at[k], c_recv.at[j], member(other))
        copy.start()
        returned.append(copy)
    loads[7].wait()
    loads[8].wait()
    for k in range(1, nj):
        other = lax.rem(j + k, nj)
        theirs = carried.at[pl.ds(pl.multiple_of(other * slab, slab), slab)]
        remote(theirs, theirs, c_send.at[k], c_recv.at[other], member(other)).wait_recv()

    def finish(i, _):
        here = pl.ds(pl.multiple_of(i * LANES, LANES), LANES)
        from_state = dot(bcc[here, N : 2 * N], carried[...], ((1,), (0,)))
        gated = ya[here, :] + yb[here, :] * from_state
        u[here, :] = (gated * gain[...]).astype(BF16)
        square = gated * gated
        total = square[:, 0:LANES]
        for part in range(1, pairs):
            total = total + square[:, part * LANES : (part + 1) * LANES]
        sq_part[here, :] = total
        return 0

    lax.fori_loop(0, length // LANES, finish, 0)

    ts = length // SUBS
    quarter = ts // 4
    half = iota((quarter, LANES), 1) < 64

    def project(p):
        col = pl.multiple_of(p * 5 * LANES, LANES)
        for begin, dest in ((0, 2 * p), (3 * LANES, 2 * p + 1)):
            part = dot(u[...], w[:, pl.ds(col + begin, 2 * LANES)], ((1,), (0,)))
            for q in range(SUBS):
                chunks[dest, q, 0:ts, :] = part[q * ts : (q + 1) * ts].astype(BF16)
        middle = dot(u[...], w[:, pl.ds(col + 2 * LANES, LANES)], ((1,), (0,)))
        turned = pltpu.roll(middle, 64, 1)
        for q in range(SUBS):
            m = [middle[q * ts + g * quarter : q * ts + (g + 1) * quarter] for g in range(4)]
            r = [turned[q * ts + g * quarter : q * ts + (g + 1) * quarter] for g in range(4)]
            even = [jnp.where(half, m[g], r[g + 1]) for g in (0, 2)]
            odd = [jnp.where(half, r[g], m[g + 1]) for g in (0, 2)]
            chunks[2 * p, q, ts : ts + quarter, :] = jnp.concatenate(even, axis=1).astype(BF16)
            chunks[2 * p + 1, q, ts : ts + quarter, :] = jnp.concatenate(odd, axis=1).astype(BF16)

    sign = 1 - 2 * c
    n_long = nz // 2
    n_short = n_long - 1

    def towards(offset):
        return lax.rem(z + offset * sign + 2 * nz, nz)

    def long_copy(source, step, q):
        return remote(
            source, long_in.at[step, q], long_send.at[step, q], long_recv.at[step, q],
            {"z": towards(1)},
        )

    def short_copy(source, step, q):
        return remote(
            source, short_in.at[step, q], short_send.at[step, q], short_recv.at[step, q],
            {"z": towards(-1)},
        )

    half_nz = nz // 2
    first = lax.div(towards(n_long), 2)

    def pair_at(offset):
        return lax.rem(first + offset * sign + 2 * half_nz, half_nz)

    def start_long(q, _):
        long_copy(chunks.at[towards(n_long), q], 0, q).start()
        return 0

    def start_short(q, _):
        short_copy(chunks.at[towards(-n_short), q], 0, q).start()
        return 0

    order = [0, 1, -1, 2][:half_nz] if half_nz > 2 else list(range(half_nz))
    project(pair_at(order[0]))
    lax.fori_loop(0, SUBS, start_long, 0)
    if half_nz > 1:
        project(pair_at(order[1]))
    if n_short:
        lax.fori_loop(0, SUBS, start_short, 0)

    squares = jnp.zeros((16, length), F32)
    for piece in split_three(sq_part[...]):
        squares = squares + dot(jnp.ones((16, LANES), BF16), piece, ((1,), (1,)))
    sq_buf[z] = squares[0:1, :]
    shared = []
    for k in range(1, nz):
        copy = remote(
            sq_buf.at[z], sq_buf.at[z], sq_send.at[k], sq_recv.at[z], {"z": lax.rem(z + k, nz)}
        )
        copy.start()
        shared.append(copy)
    for offset in order[2:]:
        project(pair_at(offset))

    for step in range(1, n_long):

        def relay(q, _, step=step):
            long_copy(long_in.at[step - 1, q], step - 1, q).wait_recv()
            long_out[step - 1, q] = (
                long_in[step - 1, q].astype(F32) + chunks[towards(n_long - step), q].astype(F32)
            ).astype(BF16)
            long_copy(long_out.at[step - 1, q], step, q).start()
            if step < n_short:
                short_copy(short_in.at[step - 1, q], step - 1, q).wait_recv()
                short_out[step - 1, q] = (
                    short_in[step - 1, q].astype(F32)
                    + chunks[towards(step - n_short), q].astype(F32)
                ).astype(BF16)
                short_copy(short_out.at[step - 1, q], step, q).start()
            return 0

        lax.fori_loop(0, SUBS, relay, 0)

    for k in range(1, nz):
        other = lax.rem(z + k, nz)
        remote(sq_buf.at[other], sq_buf.at[other], sq_send.at[k], sq_recv.at[other], {"z": other}).wait_recv()
    summed = sq_buf[0]
    for i in range(1, nz):
        summed = summed + sq_buf[i]
    high, middle, low = split_three(summed)
    which = iota((16, length), 0)
    table = jnp.where(
        which == 0,
        high.astype(F32),
        jnp.where(which == 1, middle.astype(F32), jnp.where(which == 2, low.astype(F32), 0.0)),
    ).astype(BF16)
    spread = dot(table, jnp.ones((16, LANES), BF16), ((0,), (0,)))
    rstd[...] = lax.rsqrt(spread * (1.0 / (width * nz)) + 1e-5)

    def deliver(q, _):
        long_copy(long_in.at[n_long - 1, q], n_long - 1, q).wait_recv()
        total = chunks[z, q].astype(F32) + long_in[n_long - 1, q].astype(F32)
        if n_short:
            short_copy(short_in.at[n_short - 1, q], n_short - 1, q).wait_recv()
            total = total + short_in[n_short - 1, q].astype(F32)
        base = pl.multiple_of(q * ts, ts)
        here = pl.ds(base, ts)
        scale = rstd[here, :]
        a0 = total[0:ts, 0:LANES] * scale
        a1 = total[0:ts, LANES : 2 * LANES] * scale
        b0 = total[ts : ts + quarter, 0:LANES]
        b1 = total[ts : ts + quarter, LANES : 2 * LANES]
        b = jnp.concatenate([b0, pltpu.roll(b0, 64, 1), b1, pltpu.roll(b1, 64, 1)], axis=0) * scale

        @pl.when(lax.rem(z, 2) == 0)
        def _():
            out_ref[here, 0:LANES] = a0.astype(BF16)
            out_ref[here, LANES : 2 * LANES] = a1.astype(BF16)
            out_ref[here, 2 * LANES : 2 * LANES + 64] = b[:, 0:64].astype(BF16)

        @pl.when(lax.rem(z, 2) == 1)
        def _():
            r0 = pltpu.roll(a0, 64, 1)
            r1 = pltpu.roll(a1, 64, 1)
            low_half = iota((ts, LANES), 1) < 64
            out_ref[here, 0:LANES] = jnp.where(low_half, b, r0).astype(BF16)
            out_ref[here, LANES : 2 * LANES] = jnp.where(low_half, r0, r1).astype(BF16)
            out_ref[here, 2 * LANES : 2 * LANES + 64] = r1[:, 0:64].astype(BF16)

        return 0

    lax.fori_loop(0, SUBS, deliver, 0)

    @pl.when(flat < ny * nj - 1)
    def _():
        for copy in halos:
            copy.wait_send()

    for copy in decays + totals + sent + returned + shared:
        copy.wait_send()
    for k in range(1, ny):

        @pl.when(y + k < ny)
        def _(k=k):
            remote(
                y_buf.at[y], y_buf.at[y], y_send.at[k], y_recv.at[y], {"y": lax.rem(y + k, ny)}
            ).wait_send()

    def drained(q, _):
        for step in range(n_long):
            long_copy(long_in.at[step, q], step, q).wait_send()
        for step in range(n_short):
            short_copy(short_in.at[step, q], step, q).wait_send()
        return 0

    lax.fori_loop(0, SUBS, drained, 0)


def shards(sizes, head_input, bc_input, conv_x, conv_bc, log_decay, d_skip, gate_z, norm_gain, w_out):
    ny, nx, nc, nz = sizes
    nj = nx * nc
    length, width = head_input.shape
    heads = log_decay.shape[0]
    slab = N // nj
    out_width = w_out.shape[1] // nz
    ts = length // SUBS
    rows = ts + ts // 4
    n_long = nz // 2
    n_short = n_long - 1
    dma = pltpu.SemaphoreType.DMA
    vmem = pltpu.VMEM
    scratch = [
        vmem((length, width), BF16), vmem((length, 2 * N), BF16),
        vmem((K, width), F32), vmem((K, 2 * N), F32), vmem((heads, length), F32),
        pltpu.SMEM((heads,), F32), vmem((length, width), BF16), vmem((1, width), F32),
        vmem(w_out.shape, BF16),
        dma((9,)),
        vmem((16, width), BF16), vmem((16, 2 * N), BF16), dma((2,)), dma((2,)),
        vmem((length + 8, width), F32), vmem((length + 8, 2 * N), F32),
        vmem((length, width), BF16), vmem((length, 2 * N), BF16),
        vmem((heads, 1, length), F32), vmem((length, width), F32), vmem((length, heads * LANES), F32),
        vmem((length, length), F32), vmem((length, width), BF16), vmem((N, width), BF16),
        vmem((nj, 1, width), F32), dma((nj,)), dma((nj,)),
        vmem((ny, 1, width), F32), dma((ny,)), dma((ny,)),
        vmem((nj, slab, width), BF16), dma((nj,)), dma((nj,)), vmem((nj, slab, width), F32),
        vmem((ny, slab, width), BF16), dma((ny,)), dma((ny,)),
        vmem((nj, slab, width), BF16), vmem((N, width), BF16), dma((nj,)), dma((nj,)),
        vmem((length, width), F32), vmem((length, width), F32), vmem((length, width), BF16),
        vmem((length, LANES), F32),
        vmem((nz, 1, length), F32), dma((nz,)), dma((nz,)),
        vmem((nz, SUBS, rows, 2 * LANES), BF16),
        vmem((max(n_long - 1, 1), SUBS, rows, 2 * LANES), BF16),
        vmem((max(n_short - 1, 1), SUBS, rows, 2 * LANES), BF16),
        vmem((n_long, SUBS, rows, 2 * LANES), BF16),
        vmem((max(n_short, 1), SUBS, rows, 2 * LANES), BF16),
        dma((n_long, SUBS)), dma((n_long, SUBS)),
        dma((max(n_short, 1), SUBS)), dma((max(n_short, 1), SUBS)),
        vmem((length, LANES), F32),
    ]
    return pl.pallas_call(
        functools.partial(kernel, sizes),
        out_shape=jax.ShapeDtypeStruct((length, out_width), BF16),
        in_specs=[pl.BlockSpec(memory_space=pl.ANY)] * 9,
        out_specs=pl.BlockSpec(memory_space=pltpu.VMEM),
        scratch_shapes=scratch,
        compiler_params=pltpu.CompilerParams(
            collective_id=0, has_side_effects=True, vmem_limit_bytes=60 * 1024 * 1024
        ),
        name="layer",
    )(
        head_input, bc_input, conv_x, conv_bc, log_decay, d_skip, gate_z,
        norm_gain.reshape(1, width), w_out,
    )


def solution(mesh):
    n_ctx, nz = mesh.devices.shape
    sizes = (8, 4, 2, nz) if n_ctx == 64 else (2, max(n_ctx // 4, 1), 2, nz)
    split = Mesh(mesh.devices.reshape(sizes), ("y", "x", "c", "z"))
    return jax.shard_map(
        functools.partial(shards, sizes),
        mesh=split,
        in_specs=(
            P(CTX, "z"), P(CTX, None), P(None, "z"), P(), P("z", CTX), P("z"), P(CTX, "z"),
            P("z"), P("z", None),
        ),
        out_specs=P(CTX, "z"),
        check_vma=False,
    )
```

```python
import functools

import jax
import jax.numpy as jnp
from jax import lax
from jax.experimental import pallas as pl
from jax.experimental.pallas import tpu as pltpu
from jax.sharding import Mesh
from jax.sharding import PartitionSpec as P

F32 = jnp.float32
BF16 = jnp.bfloat16
MESH = pl.DeviceIdType.MESH
N = 128
K = 4
LANES = 128
ROWS = 64
SUBS = 4
CTX = ("y", "x", "c")


def split_three(value):
    high = value.astype(BF16)
    rest = value - high.astype(F32)
    middle = rest.astype(BF16)
    low = (rest - middle.astype(F32)).astype(BF16)
    return high, middle, low


def silu(value):
    small = jnp.exp(-jnp.abs(value))
    return value * jnp.where(value >= 0, 1.0, small) / (1.0 + small)


def dot(a, b, dims):
    return lax.dot_general(a, b, (dims, ((), ())), preferred_element_type=F32)


def iota(shape, dim):
    return lax.broadcasted_iota(jnp.int32, shape, dim)


def remote(source, target, send_sem, recv_sem, device):
    return pltpu.make_async_remote_copy(
        src_ref=source,
        dst_ref=target,
        send_sem=send_sem,
        recv_sem=recv_sem,
        device_id=device,
        device_id_type=MESH,
    )


def kernel(
    sizes,
    x_hbm, bc_hbm, cx_hbm, cbc_hbm, ld_hbm, d_hbm, gate_hbm, gain_hbm, w_hbm,
    out_ref,
    x_in, bc_in, cx, cbc, ld, d_skip, gate, gain, w,
    load_sem,
    halo_x, halo_bc, halo_send, halo_recv,
    xc, bcc, crow, cum, cum2, gram, scaled, state,
    decay_row, decay_send, decay_recv,
    total_row, total_send, total_recv,
    row_buf, row_send, row_recv, prefix,
    y_buf, y_send, y_recv,
    c_out, carried, c_send, c_recv,
    ya, yb, sq_part,
    sq_buf, sq_send, sq_recv,
    wt, ut, chunks, long_out, short_out, long_in, short_in,
    long_send, long_recv, short_send, short_recv,
):
    ny, nx, nc, nz = sizes
    nj = nx * nc
    y, x, c, z = (lax.axis_index(name) for name in ("y", "x", "c", "z"))
    j = x * nc + c
    flat = y * nj + j
    slab = N // nj
    heads, length = ld.shape
    width = x_in.shape[1]
    pairs = width // LANES

    loads = [
        pltpu.make_async_copy(source, target, load_sem.at[i])
        for i, (source, target) in enumerate(
            [
                (ld_hbm, ld), (x_hbm, x_in), (bc_hbm, bc_in), (cx_hbm, cx), (cbc_hbm, cbc),
                (d_hbm, d_skip), (gate_hbm, gate), (gain_hbm, gain), (w_hbm, w),
            ]
        )
    ]
    for load in loads:
        load.start()

    def member(index):
        return {"x": lax.div(index, nc), "c": lax.rem(index, nc)}

    def at(index):
        return {"y": lax.div(index, nj), **member(lax.rem(index, nj))}

    after = at(lax.rem(flat + 1, ny * nj))
    ahead = at(lax.rem(flat + ny * nj - 1, ny * nj))

    barrier = pltpu.get_barrier_semaphore()

    def greet(device):
        pl.semaphore_signal(barrier, inc=1, device_id=device, device_id_type=MESH)

    greet(after)
    greet(ahead)
    for k in range(1, ny):
        greet({"y": lax.rem(y + k, ny)})
    for k in range(1, nz):
        greet({"z": lax.rem(z + k, nz)})
    for k in range(1, nj):
        greet(member(lax.rem(j + k, nj)))

    pl.semaphore_wait(barrier, 2 + (ny - 1) + (nz - 1) + (nj - 1))
    tail = pl.ds(length - 16, 16)
    halos = [
        remote(x_hbm.at[tail], halo_x, halo_send.at[0], halo_recv.at[0], after),
        remote(bc_hbm.at[tail], halo_bc, halo_send.at[1], halo_recv.at[1], after),
    ]

    @pl.when(flat < ny * nj - 1)
    def _():
        for copy in halos:
            copy.start()

    loads[0].wait()
    padded = jnp.concatenate([ld[...], jnp.zeros((16 - heads, length), F32)], axis=0)
    upper = (iota((length, length), 0) <= iota((length, length), 1)).astype(BF16)
    three = dot(jnp.concatenate(split_three(padded), axis=0), upper, ((1,), (0,)))
    rows = three[0:16] + (three[16:32] + three[32:48])
    stacked = jnp.concatenate(split_three(rows), axis=0)
    pick = (iota((48, width), 0) & 15) == lax.shift_right_logical(iota((48, width), 1), 6)
    cum[...] = dot(stacked, pick.astype(BF16), ((0,), (0,)))
    decay_row[j] = cum[length - 1 : length, :]

    decays = []
    for k in range(1, nj):
        other = lax.rem(j + k, nj)
        copy = remote(
            decay_row.at[j], decay_row.at[j], decay_send.at[k], decay_recv.at[j], member(other)
        )
        copy.start()
        decays.append(copy)

    for load in loads[1:5]:
        load.wait()

    def filtered(block, taps):
        total = taps[K - 1 : K, :] * block[16:]
        for tap in range(K - 1):
            total = total + taps[tap : tap + 1, :] * pltpu.roll(block, K - 1 - tap, 0)[16:]
        return silu(total).astype(BF16)

    def convolve(here, block_x, block_bc):
        conv = filtered(block_x.astype(F32), cx)
        xc[here, :] = conv
        bcc[here, :] = filtered(block_bc.astype(F32), cbc)
        weight = jnp.exp(cum[length - 1 : length, :] - cum[here, :])
        scaled[here, :] = (conv.astype(F32) * weight).astype(BF16)

    def convolve_at(i, _):
        r = pl.multiple_of(i * ROWS, ROWS)
        block = pl.ds(pl.multiple_of(r - 16, 16), ROWS + 16)
        convolve(pl.ds(r, ROWS), x_in[block, :], bc_in[block, :])
        return 0

    lax.fori_loop(1, length // ROWS, convolve_at, 0)
    later = dot(bcc[ROWS:length, 0:N], scaled[ROWS:length, :], ((0,), (0,)))

    @pl.when(flat == 0)
    def _():
        halo_x[...] = jnp.zeros((16, width), BF16)
        halo_bc[...] = jnp.zeros((16, 2 * N), BF16)

    @pl.when(flat > 0)
    def _():
        for copy in halos:
            copy.wait_recv()

    convolve(
        slice(0, ROWS),
        jnp.concatenate([halo_x[...], x_in[0:ROWS, :]], axis=0),
        jnp.concatenate([halo_bc[...], bc_in[0:ROWS, :]], axis=0),
    )

    state[...] = (later + dot(bcc[0:ROWS, 0:N], scaled[0:ROWS, :], ((0,), (0,)))).astype(BF16)
    row_buf[j] = state[pl.ds(pl.multiple_of(j * slab, slab), slab), :]
    sent = []
    for k in range(1, nj):
        other = lax.rem(j + k, nj)
        copy = remote(
            state.at[pl.ds(pl.multiple_of(other * slab, slab), slab)],
            row_buf.at[j],
            row_send.at[k],
            row_recv.at[j],
            member(other),
        )
        copy.start()
        sent.append(copy)

    for k in range(1, nj):
        other = lax.rem(j + k, nj)
        remote(
            decay_row.at[other], decay_row.at[other], decay_send.at[k], decay_recv.at[other],
            member(other),
        ).wait_recv()
    whole = decay_row[0]
    for i in range(1, nj):
        whole = whole + decay_row[i]
    total_row[y] = whole
    totals = []
    for k in range(1, ny):
        copy = remote(
            total_row.at[y], total_row.at[y], total_send.at[k], total_recv.at[y],
            {"y": lax.rem(y + k, ny)},
        )
        copy.start()
        totals.append(copy)

    for h in range(heads):
        crow[h] = rows[h : h + 1]
    wide = heads * LANES
    pick2 = (iota((48, wide), 0) & 15) == lax.shift_right_logical(iota((48, wide), 1), 7)
    cum2[...] = dot(stacked, pick2.astype(BF16), ((0,), (0,)))
    gram[...] = dot(bcc[:, N : 2 * N], bcc[:, 0:N], ((1,), (1,)))
    left = iota((LANES, LANES), 1) < 64
    causal = iota((LANES, LANES), 0) >= iota((LANES, LANES), 1)
    loads[5].wait()

    def local_pair(i, _):
        lanes = pl.ds(pl.multiple_of(i * LANES, LANES), LANES)
        for block in range(length // LANES):
            t = slice(block * LANES, (block + 1) * LANES)
            results = []
            for side in range(2):
                h = 2 * i + side
                here = cum2[t, pl.ds(pl.multiple_of(h * LANES, LANES), LANES)]
                parts = []
                for other in range(block + 1):
                    s = slice(other * LANES, (other + 1) * LANES)
                    spread = here - crow[h, :, s]
                    if other == block:
                        part = jnp.where(causal, gram[t, s] * jnp.exp(jnp.minimum(spread, 0.0)), 0.0)
                    else:
                        part = gram[t, s] * jnp.exp(spread)
                    parts.append(part.astype(BF16))
                mixing = parts[0] if block == 0 else jnp.concatenate(parts, axis=1)
                results.append(dot(mixing, xc[0 : (block + 1) * LANES, lanes], ((1,), (0,))))
            skip = jnp.where(left, d_skip[2 * i], d_skip[2 * i + 1])
            ya[t, lanes] = jnp.where(left, results[0], results[1]) + skip * xc[t, lanes].astype(F32)
        return 0

    lax.fori_loop(0, 2, local_pair, 0)

    for k in range(1, nj):
        other = lax.rem(j + k, nj)
        remote(
            row_buf.at[other], row_buf.at[other], row_send.at[k], row_recv.at[other], member(other)
        ).wait_recv()
    running = jnp.zeros((slab, width), F32)
    for i in range(nj):
        prefix[i] = running
        running = jnp.exp(decay_row[i]) * running + row_buf[i].astype(F32)
    y_buf[y] = running.astype(BF16)
    for k in range(1, ny):

        @pl.when(y + k < ny)
        def _(k=k):
            remote(
                y_buf.at[y], y_buf.at[y], y_send.at[k], y_recv.at[y], {"y": lax.rem(y + k, ny)}
            ).start()

    lax.fori_loop(2, pairs, local_pair, 0)

    loads[6].wait()

    def gates(i, _):
        here = pl.ds(pl.multiple_of(i * ROWS, ROWS), ROWS)
        factor = silu(gate[here, :].astype(F32))
        ya[here, :] = ya[here, :] * factor
        yb[here, :] = jnp.exp(cum[here, :]) * factor
        return 0

    lax.fori_loop(0, length // ROWS, gates, 0)

    loads[8].wait()

    def turn(i, _):
        here = pl.ds(pl.multiple_of(i * LANES, LANES), LANES)
        wt[here, :] = w[:, here].T
        return 0

    blocks = w.shape[1] // LANES
    lax.fori_loop(0, blocks * 5 // 8, turn, 0)

    for k in range(1, ny):
        other = lax.rem(y + k, ny)
        remote(
            total_row.at[other], total_row.at[other], total_send.at[k], total_recv.at[other],
            {"y": other},
        ).wait_recv()
    for k in range(1, ny):

        @pl.when(y >= k)
        def _(k=k):
            other = lax.rem(y - k + ny, ny)
            remote(
                y_buf.at[other], y_buf.at[other], y_send.at[k], y_recv.at[other], {"y": other}
            ).wait_recv()

    def earlier(i, total):
        return jnp.exp(total_row[i]) * total + y_buf[i].astype(F32)

    base = lax.fori_loop(0, y, earlier, jnp.zeros((slab, width), F32))
    fade = jnp.zeros((1, width), F32)
    for i in range(nj):
        c_out[i] = (jnp.exp(fade) * base + prefix[i]).astype(BF16)
        fade = fade + decay_row[i]
    mine = pl.ds(pl.multiple_of(j * slab, slab), slab)
    carried[mine, :] = c_out[j]
    returned = []
    for k in range(1, nj):
        other = lax.rem(j + k, nj)
        copy = remote(c_out.at[other], carried.at[mine], c_send.at[k], c_recv.at[j], member(other))
        copy.start()
        returned.append(copy)
    loads[7].wait()
    lax.fori_loop(blocks * 5 // 8, blocks, turn, 0)
    amount = gain[...].reshape(1, width)
    for k in range(1, nj):
        other = lax.rem(j + k, nj)
        theirs = carried.at[pl.ds(pl.multiple_of(other * slab, slab), slab)]
        remote(theirs, theirs, c_send.at[k], c_recv.at[other], member(other)).wait_recv()

    def finish(i, _):
        here = pl.ds(pl.multiple_of(i * LANES, LANES), LANES)
        from_state = dot(bcc[here, N : 2 * N], carried[...], ((1,), (0,)))
        gated = ya[here, :] + yb[here, :] * from_state
        ut[:, here] = (gated * amount).astype(BF16).T
        square = gated * gated
        total = square[:, 0:LANES]
        for part in range(1, pairs):
            total = total + square[:, part * LANES : (part + 1) * LANES]
        sq_part[here, :] = total
        return 0

    lax.fori_loop(0, length // LANES, finish, 0)

    rows_out = out_ref.shape[0]
    piece = rows_out // SUBS

    def project(d):
        here = pl.ds(pl.multiple_of(d * rows_out, 64), rows_out)
        part = dot(wt[here, :], ut[...], ((1,), (0,))).astype(BF16)
        for q in range(SUBS):
            chunks[d, q] = part[q * piece : (q + 1) * piece]

    sign = 1 - 2 * c
    n_long = nz // 2
    n_short = n_long - 1

    def towards(offset):
        return lax.rem(z + offset * sign + 2 * nz, nz)

    def long_copy(source, step, q):
        return remote(
            source, long_in.at[step, q], long_send.at[step, q], long_recv.at[step, q],
            {"z": towards(1)},
        )

    def short_copy(source, step, q):
        return remote(
            source, short_in.at[step, q], short_send.at[step, q], short_recv.at[step, q],
            {"z": towards(-1)},
        )

    def start_long(q, _):
        long_copy(chunks.at[towards(n_long), q], 0, q).start()
        return 0

    def start_short(q, _):
        short_copy(chunks.at[towards(-n_short), q], 0, q).start()
        return 0

    project(towards(n_long))
    lax.fori_loop(0, SUBS, start_long, 0)
    if n_short:
        project(towards(-n_short))
        lax.fori_loop(0, SUBS, start_short, 0)

    squares = jnp.zeros((16, length), F32)
    for term in split_three(sq_part[...]):
        squares = squares + dot(jnp.ones((16, LANES), BF16), term, ((1,), (1,)))
    sq_buf[z] = squares[0:1, :]
    shared = []
    for k in range(1, nz):
        copy = remote(
            sq_buf.at[z], sq_buf.at[z], sq_send.at[k], sq_recv.at[z], {"z": lax.rem(z + k, nz)}
        )
        copy.start()
        shared.append(copy)

    for step in range(1, n_long):
        project(towards(n_long - step))
        if step < n_short:
            project(towards(step - n_short))
    project(z)

    for step in range(1, n_long):

        def relay(q, _, step=step):
            long_copy(long_in.at[step - 1, q], step - 1, q).wait_recv()
            long_out[step - 1, q] = (
                long_in[step - 1, q].astype(F32) + chunks[towards(n_long - step), q].astype(F32)
            ).astype(BF16)
            long_copy(long_out.at[step - 1, q], step, q).start()
            if step < n_short:
                short_copy(short_in.at[step - 1, q], step - 1, q).wait_recv()
                short_out[step - 1, q] = (
                    short_in[step - 1, q].astype(F32)
                    + chunks[towards(step - n_short), q].astype(F32)
                ).astype(BF16)
                short_copy(short_out.at[step - 1, q], step, q).start()
            return 0

        lax.fori_loop(0, SUBS, relay, 0)

    for k in range(1, nz):
        other = lax.rem(z + k, nz)
        remote(sq_buf.at[other], sq_buf.at[other], sq_send.at[k], sq_recv.at[other], {"z": other}).wait_recv()
    summed = sq_buf[0]
    for i in range(1, nz):
        summed = summed + sq_buf[i]
    scale = lax.rsqrt(summed * (1.0 / (width * nz)) + 1e-5)

    def deliver(q, _):
        long_copy(long_in.at[n_long - 1, q], n_long - 1, q).wait_recv()
        total = chunks[z, q].astype(F32) + long_in[n_long - 1, q].astype(F32)
        if n_short:
            short_copy(short_in.at[n_short - 1, q], n_short - 1, q).wait_recv()
            total = total + short_in[n_short - 1, q].astype(F32)
        out_ref[pl.ds(pl.multiple_of(q * piece, piece), piece), :] = (total * scale).astype(BF16)
        return 0

    lax.fori_loop(0, SUBS, deliver, 0)

    @pl.when(flat < ny * nj - 1)
    def _():
        for copy in halos:
            copy.wait_send()

    for copy in decays + totals + sent + returned + shared:
        copy.wait_send()
    for k in range(1, ny):

        @pl.when(y + k < ny)
        def _(k=k):
            remote(
                y_buf.at[y], y_buf.at[y], y_send.at[k], y_recv.at[y], {"y": lax.rem(y + k, ny)}
            ).wait_send()

    def drained(q, _):
        for step in range(n_long):
            long_copy(long_in.at[step, q], step, q).wait_send()
        for step in range(n_short):
            short_copy(short_in.at[step, q], step, q).wait_send()
        return 0

    lax.fori_loop(0, SUBS, drained, 0)


def shards(sizes, head_input, bc_input, conv_x, conv_bc, log_decay, d_skip, gate_z, norm_gain, w_out):
    ny, nx, nc, nz = sizes
    nj = nx * nc
    length, width = head_input.shape
    heads = log_decay.shape[0]
    slab = N // nj
    out_width = w_out.shape[1] // nz
    piece = out_width // SUBS
    n_long = nz // 2
    n_short = n_long - 1
    dma = pltpu.SemaphoreType.DMA
    vmem = pltpu.VMEM
    scratch = [
        vmem((length, width), BF16), vmem((length, 2 * N), BF16),
        vmem((K, width), F32), vmem((K, 2 * N), F32), vmem((heads, length), F32),
        pltpu.SMEM((heads,), F32), vmem((length, width), BF16), vmem((width,), F32),
        vmem(w_out.shape, BF16),
        dma((9,)),
        vmem((16, width), BF16), vmem((16, 2 * N), BF16), dma((2,)), dma((2,)),
        vmem((length, width), BF16), vmem((length, 2 * N), BF16),
        vmem((heads, 1, length), F32), vmem((length, width), F32), vmem((length, heads * LANES), F32),
        vmem((length, length), F32), vmem((length, width), BF16), vmem((N, width), BF16),
        vmem((nj, 1, width), F32), dma((nj,)), dma((nj,)),
        vmem((ny, 1, width), F32), dma((ny,)), dma((ny,)),
        vmem((nj, slab, width), BF16), dma((nj,)), dma((nj,)), vmem((nj, slab, width), F32),
        vmem((ny, slab, width), BF16), dma((ny,)), dma((ny,)),
        vmem((nj, slab, width), BF16), vmem((N, width), BF16), dma((nj,)), dma((nj,)),
        vmem((length, width), F32), vmem((length, width), F32), vmem((length, LANES), F32),
        vmem((nz, 1, length), F32), dma((nz,)), dma((nz,)),
        vmem(w_out.shape[::-1], BF16), vmem((width, length), BF16),
        vmem((nz, SUBS, piece, length), BF16),
        vmem((max(n_long - 1, 1), SUBS, piece, length), BF16),
        vmem((max(n_short - 1, 1), SUBS, piece, length), BF16),
        vmem((n_long, SUBS, piece, length), BF16),
        vmem((max(n_short, 1), SUBS, piece, length), BF16),
        dma((n_long, SUBS)), dma((n_long, SUBS)),
        dma((max(n_short, 1), SUBS)), dma((max(n_short, 1), SUBS)),
    ]
    return pl.pallas_call(
        functools.partial(kernel, sizes),
        out_shape=jax.ShapeDtypeStruct((out_width, length), BF16),
        in_specs=[pl.BlockSpec(memory_space=pl.ANY)] * 9,
        out_specs=pl.BlockSpec(memory_space=pltpu.VMEM),
        scratch_shapes=scratch,
        compiler_params=pltpu.CompilerParams(
            collective_id=0, has_side_effects=True, vmem_limit_bytes=60 * 1024 * 1024
        ),
        name="layer",
    )(
        head_input, bc_input, conv_x, conv_bc, log_decay, d_skip, gate_z,
        norm_gain, w_out,
    ).T


def solution(mesh):
    n_ctx, nz = mesh.devices.shape
    sizes = (8, 4, 2, nz) if n_ctx == 64 else (2, max(n_ctx // 4, 1), 2, nz)
    split = Mesh(mesh.devices.reshape(sizes), ("y", "x", "c", "z"))
    return jax.shard_map(
        functools.partial(shards, sizes),
        mesh=split,
        in_specs=(
            P(CTX, "z"), P(CTX, None), P(None, "z"), P(), P("z", CTX), P("z"), P(CTX, "z"),
            P("z"), P("z", None),
        ),
        out_specs=P(CTX, "z"),
        check_vma=False,
    )
```

```python
import functools

import jax
import jax.numpy as jnp
from jax import lax
from jax.experimental import pallas as pl
from jax.experimental.pallas import tpu as pltpu
from jax.sharding import Mesh
from jax.sharding import PartitionSpec as P

F32 = jnp.float32
BF16 = jnp.bfloat16
MESH = pl.DeviceIdType.MESH
N = 128
K = 4
LANES = 128
ROWS = 64
SUBS = 4
CTX = ("y", "x", "c")


def split_three(value):
    high = value.astype(BF16)
    rest = value - high.astype(F32)
    middle = rest.astype(BF16)
    low = (rest - middle.astype(F32)).astype(BF16)
    return high, middle, low


def silu(value):
    half = 0.5 * value
    return half + half * jnp.tanh(half)


def dot(a, b, dims):
    return lax.dot_general(a, b, (dims, ((), ())), preferred_element_type=F32)


def iota(shape, dim):
    return lax.broadcasted_iota(jnp.int32, shape, dim)


def remote(source, target, send_sem, recv_sem, device):
    return pltpu.make_async_remote_copy(
        src_ref=source,
        dst_ref=target,
        send_sem=send_sem,
        recv_sem=recv_sem,
        device_id=device,
        device_id_type=MESH,
    )


def kernel(
    sizes,
    x_hbm, bc_hbm, cx_hbm, cbc_hbm, ld_hbm, d_hbm, gate_hbm, gain_hbm, w_hbm,
    out_ref,
    x_in, bc_in, cx, cbc, ld, d_skip, gate, gain, w,
    load_sem,
    halo_x, halo_bc, halo_send, halo_recv,
    xc, bcc, crow, cum, cum2, gram, scaled, later, state,
    decay_row, decay_send, decay_recv,
    total_row, total_send, total_recv,
    row_buf, row_send, row_recv, prefix,
    y_buf, y_send, y_recv,
    c_out, carried, c_send, c_recv,
    ya, yb, sq_part,
    sq_buf, sq_send, sq_recv,
    wt, ut, chunks, long_out, short_out, long_in, short_in,
    long_send, long_recv, short_send, short_recv,
):
    ny, nx, nc, nz = sizes
    nj = nx * nc
    y, x, c, z = (lax.axis_index(name) for name in ("y", "x", "c", "z"))
    j = x * nc + c
    flat = y * nj + j
    slab = N // nj
    heads, length = ld.shape
    width = x_in.shape[1]
    pairs = width // LANES
    cut = (pairs + 1) // 2 * LANES
    halves = [slice(0, cut), slice(cut, width)]
    row_steps = sorted(range(1, nj), key=lambda k: -min(k, nj - k))
    y_steps = sorted(range(1, ny), key=lambda k: -min(k, ny - k))

    loads = [
        pltpu.make_async_copy(source, target, load_sem.at[i])
        for i, (source, target) in enumerate(
            [
                (ld_hbm, ld), (x_hbm, x_in), (bc_hbm, bc_in), (cx_hbm, cx), (cbc_hbm, cbc),
                (d_hbm, d_skip), (gate_hbm, gate), (gain_hbm, gain), (w_hbm, w),
            ]
        )
    ]
    for load in loads:
        load.start()

    def member(index):
        return {"x": lax.div(index, nc), "c": lax.rem(index, nc)}

    def at(index):
        return {"y": lax.div(index, nj), **member(lax.rem(index, nj))}

    after = at(lax.rem(flat + 1, ny * nj))
    ahead = at(lax.rem(flat + ny * nj - 1, ny * nj))

    barrier = pltpu.get_barrier_semaphore()

    def greet(device):
        pl.semaphore_signal(barrier, inc=1, device_id=device, device_id_type=MESH)

    greet(after)
    greet(ahead)
    for k in range(1, ny):
        greet({"y": lax.rem(y + k, ny)})
    for k in range(1, nz):
        greet({"z": lax.rem(z + k, nz)})
    for k in range(1, nj):
        greet(member(lax.rem(j + k, nj)))

    pl.semaphore_wait(barrier, 2 + (ny - 1) + (nz - 1) + (nj - 1))
    tail = pl.ds(length - 16, 16)
    halos = [
        remote(x_hbm.at[tail], halo_x, halo_send.at[0], halo_recv.at[0], after),
        remote(bc_hbm.at[tail], halo_bc, halo_send.at[1], halo_recv.at[1], after),
    ]

    @pl.when(flat < ny * nj - 1)
    def _():
        for copy in halos:
            copy.start()

    loads[0].wait()
    padded = jnp.concatenate([ld[...], jnp.zeros((16 - heads, length), F32)], axis=0)
    upper = (iota((length, length), 0) <= iota((length, length), 1)).astype(BF16)
    three = dot(jnp.concatenate(split_three(padded), axis=0), upper, ((1,), (0,)))
    rows = three[0:16] + (three[16:32] + three[32:48])
    stacked = jnp.concatenate(split_three(rows), axis=0)
    pick = (iota((48, width), 0) & 15) == lax.shift_right_logical(iota((48, width), 1), 6)
    cum[...] = dot(stacked, pick.astype(BF16), ((0,), (0,)))
    decay_row[j] = cum[length - 1 : length, :]

    decays = []
    for k in range(1, nj):
        other = lax.rem(j + k, nj)
        copy = remote(
            decay_row.at[j], decay_row.at[j], decay_send.at[k], decay_recv.at[j], member(other)
        )
        copy.start()
        decays.append(copy)

    for load in loads[1:5]:
        load.wait()

    def filtered(block, taps):
        total = taps[K - 1 : K, :] * block[16:]
        for tap in range(K - 1):
            total = total + taps[tap : tap + 1, :] * pltpu.roll(block, K - 1 - tap, 0)[16:]
        return silu(total).astype(BF16)

    def convolve(here, block_x, block_bc):
        conv = filtered(block_x.astype(F32), cx)
        xc[here, :] = conv
        bcc[here, :] = filtered(block_bc.astype(F32), cbc)
        weight = jnp.exp(cum[length - 1 : length, :] - cum[here, :])
        scaled[here, :] = (conv.astype(F32) * weight).astype(BF16)

    def convolve_at(i, _):
        r = pl.multiple_of(i * ROWS, ROWS)
        block = pl.ds(pl.multiple_of(r - 16, 16), ROWS + 16)
        convolve(pl.ds(r, ROWS), x_in[block, :], bc_in[block, :])
        return 0

    lax.fori_loop(1, length // ROWS, convolve_at, 0)
    later[...] = dot(bcc[ROWS:length, 0:N], scaled[ROWS:length, :], ((0,), (0,)))

    @pl.when(flat == 0)
    def _():
        halo_x[...] = jnp.zeros((16, width), BF16)
        halo_bc[...] = jnp.zeros((16, 2 * N), BF16)

    @pl.when(flat > 0)
    def _():
        for copy in halos:
            copy.wait_recv()

    convolve(
        slice(0, ROWS),
        jnp.concatenate([halo_x[...], x_in[0:ROWS, :]], axis=0),
        jnp.concatenate([halo_bc[...], bc_in[0:ROWS, :]], axis=0),
    )

    def slice_of(index):
        return pl.ds(pl.multiple_of(index * slab, slab), slab)

    sent = []
    for half, lanes in enumerate(halves):
        first = dot(bcc[0:ROWS, 0:N], scaled[0:ROWS, lanes], ((0,), (0,)))
        state[:, lanes] = (later[:, lanes] + first).astype(BF16)
        for k in row_steps:
            other = lax.rem(j + k, nj)
            copy = remote(
                state.at[slice_of(other), lanes],
                row_buf.at[j, :, lanes],
                row_send.at[half, k],
                row_recv.at[half, j],
                member(other),
            )
            copy.start()
            sent.append(copy)
        row_buf[j, :, lanes] = state[slice_of(j), lanes]

    for k in range(1, nj):
        other = lax.rem(j + k, nj)
        remote(
            decay_row.at[other], decay_row.at[other], decay_send.at[k], decay_recv.at[other],
            member(other),
        ).wait_recv()
    whole = decay_row[0]
    for i in range(1, nj):
        whole = whole + decay_row[i]
    total_row[y] = whole
    totals = []
    for k in range(1, ny):
        copy = remote(
            total_row.at[y], total_row.at[y], total_send.at[k], total_recv.at[y],
            {"y": lax.rem(y + k, ny)},
        )
        copy.start()
        totals.append(copy)

    for h in range(heads):
        crow[h] = rows[h : h + 1]
    wide = heads * LANES
    pick2 = (iota((48, wide), 0) & 15) == lax.shift_right_logical(iota((48, wide), 1), 7)
    cum2[...] = dot(stacked, pick2.astype(BF16), ((0,), (0,)))
    gram[...] = dot(bcc[:, N : 2 * N], bcc[:, 0:N], ((1,), (1,)))
    left = iota((LANES, LANES), 1) < 64
    causal = iota((LANES, LANES), 0) >= iota((LANES, LANES), 1)
    loads[5].wait()

    def local_pair(i, _):
        lanes = pl.ds(pl.multiple_of(i * LANES, LANES), LANES)
        for block in range(length // LANES):
            t = slice(block * LANES, (block + 1) * LANES)
            results = []
            for side in range(2):
                h = 2 * i + side
                here = cum2[t, pl.ds(pl.multiple_of(h * LANES, LANES), LANES)]
                parts = []
                for other in range(block + 1):
                    s = slice(other * LANES, (other + 1) * LANES)
                    spread = here - crow[h, :, s]
                    if other == block:
                        part = jnp.where(causal, gram[t, s] * jnp.exp(jnp.minimum(spread, 0.0)), 0.0)
                    else:
                        part = gram[t, s] * jnp.exp(spread)
                    parts.append(part.astype(BF16))
                mixing = parts[0] if block == 0 else jnp.concatenate(parts, axis=1)
                results.append(dot(mixing, xc[0 : (block + 1) * LANES, lanes], ((1,), (0,))))
            skip = jnp.where(left, d_skip[2 * i], d_skip[2 * i + 1])
            ya[t, lanes] = jnp.where(left, results[0], results[1]) + skip * xc[t, lanes].astype(F32)
        return 0

    lax.fori_loop(0, 2, local_pair, 0)

    def y_copy(half, k):
        lanes = halves[half]
        return remote(
            y_buf.at[y, :, lanes], y_buf.at[y, :, lanes], y_send.at[half, k], y_recv.at[half, y],
            {"y": lax.rem(y + k, ny)},
        )

    for half, lanes in enumerate(halves):
        for k in row_steps:
            other = lax.rem(j + k, nj)
            theirs = row_buf.at[other, :, lanes]
            remote(
                theirs, theirs, row_send.at[half, k], row_recv.at[half, other], member(other)
            ).wait_recv()
        running = jnp.zeros((slab, lanes.stop - lanes.start), F32)
        for i in range(nj):
            prefix[i, :, lanes] = running
            running = jnp.exp(decay_row[i, :, lanes]) * running
            running = running + row_buf[i, :, lanes].astype(F32)
        y_buf[y, :, lanes] = running.astype(BF16)
        for k in y_steps:

            @pl.when(y + k < ny)
            def _(half=half, k=k):
                y_copy(half, k).start()

    lax.fori_loop(2, pairs, local_pair, 0)

    loads[6].wait()

    def gates(i, _):
        here = pl.ds(pl.multiple_of(i * ROWS, ROWS), ROWS)
        factor = silu(gate[here, :].astype(F32))
        ya[here, :] = ya[here, :] * factor
        yb[here, :] = jnp.exp(cum[here, :]) * factor
        return 0

    lax.fori_loop(0, length // ROWS, gates, 0)

    loads[8].wait()

    def turn(i, _):
        here = pl.ds(pl.multiple_of(i * LANES, LANES), LANES)
        wt[here, :] = w[:, here].T
        return 0

    blocks = w.shape[1] // LANES
    lax.fori_loop(0, blocks * 5 // 8, turn, 0)

    for k in range(1, ny):
        other = lax.rem(y + k, ny)
        remote(
            total_row.at[other], total_row.at[other], total_send.at[k], total_recv.at[other],
            {"y": other},
        ).wait_recv()
    returned = []
    for half, lanes in enumerate(halves):
        for k in y_steps:

            @pl.when(y >= k)
            def _(half=half, lanes=lanes, k=k):
                other = lax.rem(y - k + ny, ny)
                theirs = y_buf.at[other, :, lanes]
                remote(
                    theirs, theirs, y_send.at[half, k], y_recv.at[half, other], {"y": other}
                ).wait_recv()

        def earlier(i, total, lanes=lanes):
            return jnp.exp(total_row[i, :, lanes]) * total + y_buf[i, :, lanes].astype(F32)

        part_width = lanes.stop - lanes.start
        base = lax.fori_loop(0, y, earlier, jnp.zeros((slab, part_width), F32))
        fade = jnp.zeros((1, part_width), F32)
        for i in range(nj):
            c_out[i, :, lanes] = (jnp.exp(fade) * base + prefix[i, :, lanes]).astype(BF16)
            fade = fade + decay_row[i, :, lanes]
        for k in row_steps:
            other = lax.rem(j + k, nj)
            copy = remote(
                c_out.at[other, :, lanes], carried.at[slice_of(j), lanes], c_send.at[half, k],
                c_recv.at[half, j], member(other),
            )
            copy.start()
            returned.append(copy)
        carried[slice_of(j), lanes] = c_out[j, :, lanes]

    loads[7].wait()
    lax.fori_loop(blocks * 5 // 8, blocks, turn, 0)
    amount = gain[...].reshape(1, width)

    def await_carried(half):
        for k in row_steps:
            other = lax.rem(j + k, nj)
            theirs = carried.at[slice_of(other), halves[half]]
            remote(
                theirs, theirs, c_send.at[half, k], c_recv.at[half, other], member(other)
            ).wait_recv()

    def finish(half, here):
        lanes = halves[half]
        from_state = dot(bcc[here, N : 2 * N], carried[:, lanes], ((1,), (0,)))
        gated = ya[here, lanes] + yb[here, lanes] * from_state
        ut[lanes, here] = (gated * amount[:, lanes]).astype(BF16).T
        square = gated * gated
        total = square[:, 0:LANES]
        for begin in range(LANES, lanes.stop - lanes.start, LANES):
            total = total + square[:, begin : begin + LANES]
        sq_part[here, :] = total if half == 0 else sq_part[here, :] + total

    def finish_first(i, _):
        finish(0, pl.ds(pl.multiple_of(i * LANES, LANES), LANES))
        return 0

    await_carried(0)
    lax.fori_loop(0, length // LANES, finish_first, 0)

    rows_out = out_ref.shape[0]
    piece = length // SUBS

    def tokens(q):
        return pl.ds(pl.multiple_of(q * piece, piece), piece)

    def project_piece(d, q):
        here = pl.ds(pl.multiple_of(d * rows_out, 64), rows_out)
        chunks[d, q] = dot(wt[here, :], ut[:, tokens(q)], ((1,), (0,))).astype(BF16)

    def project(d):
        here = pl.ds(pl.multiple_of(d * rows_out, 64), rows_out)
        part = dot(wt[here, :], ut[...], ((1,), (0,))).astype(BF16)
        for q in range(SUBS):
            chunks[d, q] = part[:, q * piece : (q + 1) * piece]

    sign = 1 - 2 * c
    n_long = nz // 2
    n_short = n_long - 1

    def towards(offset):
        return lax.rem(z + offset * sign + 2 * nz, nz)

    def long_copy(source, step, q):
        return remote(
            source, long_in.at[step, q], long_send.at[step, q], long_recv.at[step, q],
            {"z": towards(1)},
        )

    def short_copy(source, step, q):
        return remote(
            source, short_in.at[step, q], short_send.at[step, q], short_recv.at[step, q],
            {"z": towards(-1)},
        )

    def begin(q, _):
        finish(1, tokens(q))
        project_piece(towards(n_long), q)
        long_copy(chunks.at[towards(n_long), q], 0, q).start()
        if n_short:
            project_piece(towards(-n_short), q)
            short_copy(chunks.at[towards(-n_short), q], 0, q).start()
        return 0

    await_carried(1)
    lax.fori_loop(0, SUBS, begin, 0)

    squares = jnp.zeros((16, length), F32)
    for term in split_three(sq_part[...]):
        squares = squares + dot(jnp.ones((16, LANES), BF16), term, ((1,), (1,)))
    sq_buf[z] = squares[0:1, :]
    shared = []
    for k in range(1, nz):
        copy = remote(
            sq_buf.at[z], sq_buf.at[z], sq_send.at[k], sq_recv.at[z], {"z": lax.rem(z + k, nz)}
        )
        copy.start()
        shared.append(copy)

    for step in range(1, n_long):
        project(towards(n_long - step))
        if step < n_short:
            project(towards(step - n_short))
    project(z)

    for step in range(1, n_long):

        def relay(q, _, step=step):
            long_copy(long_in.at[step - 1, q], step - 1, q).wait_recv()
            long_out[step - 1, q] = (
                long_in[step - 1, q].astype(F32) + chunks[towards(n_long - step), q].astype(F32)
            ).astype(BF16)
            long_copy(long_out.at[step - 1, q], step, q).start()
            if step < n_short:
                short_copy(short_in.at[step - 1, q], step - 1, q).wait_recv()
                short_out[step - 1, q] = (
                    short_in[step - 1, q].astype(F32)
                    + chunks[towards(step - n_short), q].astype(F32)
                ).astype(BF16)
                short_copy(short_out.at[step - 1, q], step, q).start()
            return 0

        lax.fori_loop(0, SUBS, relay, 0)

    for k in range(1, nz):
        other = lax.rem(z + k, nz)
        remote(sq_buf.at[other], sq_buf.at[other], sq_send.at[k], sq_recv.at[other], {"z": other}).wait_recv()
    def deliver(q, _):
        long_copy(long_in.at[n_long - 1, q], n_long - 1, q).wait_recv()
        total = chunks[z, q].astype(F32) + long_in[n_long - 1, q].astype(F32)
        if n_short:
            short_copy(short_in.at[n_short - 1, q], n_short - 1, q).wait_recv()
            total = total + short_in[n_short - 1, q].astype(F32)
        summed = sq_buf[0, :, tokens(q)]
        for i in range(1, nz):
            summed = summed + sq_buf[i, :, tokens(q)]
        scale = lax.rsqrt(summed * (1.0 / (width * nz)) + 1e-5)
        out_ref[:, tokens(q)] = (total * scale).astype(BF16)
        return 0

    lax.fori_loop(0, SUBS, deliver, 0)

    @pl.when(flat < ny * nj - 1)
    def _():
        for copy in halos:
            copy.wait_send()

    for copy in decays + totals + sent + returned + shared:
        copy.wait_send()
    for half in range(2):
        for k in y_steps:

            @pl.when(y + k < ny)
            def _(half=half, k=k):
                y_copy(half, k).wait_send()

    def drained(q, _):
        for step in range(n_long):
            long_copy(long_in.at[step, q], step, q).wait_send()
        for step in range(n_short):
            short_copy(short_in.at[step, q], step, q).wait_send()
        return 0

    lax.fori_loop(0, SUBS, drained, 0)


def shards(sizes, head_input, bc_input, conv_x, conv_bc, log_decay, d_skip, gate_z, norm_gain, w_out):
    ny, nx, nc, nz = sizes
    nj = nx * nc
    length, width = head_input.shape
    heads = log_decay.shape[0]
    slab = N // nj
    out_width = w_out.shape[1] // nz
    piece = length // SUBS
    n_long = nz // 2
    n_short = n_long - 1
    dma = pltpu.SemaphoreType.DMA
    vmem = pltpu.VMEM
    scratch = [
        vmem((length, width), BF16), vmem((length, 2 * N), BF16),
        vmem((K, width), F32), vmem((K, 2 * N), F32), vmem((heads, length), F32),
        pltpu.SMEM((heads,), F32), vmem((length, width), BF16), vmem((width,), F32),
        vmem(w_out.shape, BF16),
        dma((9,)),
        vmem((16, width), BF16), vmem((16, 2 * N), BF16), dma((2,)), dma((2,)),
        vmem((length, width), BF16), vmem((length, 2 * N), BF16),
        vmem((heads, 1, length), F32), vmem((length, width), F32), vmem((length, heads * LANES), F32),
        vmem((length, length), F32), vmem((length, width), BF16),
        vmem((N, width), F32), vmem((N, width), BF16),
        vmem((nj, 1, width), F32), dma((nj,)), dma((nj,)),
        vmem((ny, 1, width), F32), dma((ny,)), dma((ny,)),
        vmem((nj, slab, width), BF16), dma((2, nj)), dma((2, nj)), vmem((nj, slab, width), F32),
        vmem((ny, slab, width), BF16), dma((2, ny)), dma((2, ny)),
        vmem((nj, slab, width), BF16), vmem((N, width), BF16), dma((2, nj)), dma((2, nj)),
        vmem((length, width), F32), vmem((length, width), F32), vmem((length, LANES), F32),
        vmem((nz, 1, length), F32), dma((nz,)), dma((nz,)),
        vmem(w_out.shape[::-1], BF16), vmem((width, length), BF16),
        vmem((nz, SUBS, out_width, piece), BF16),
        vmem((max(n_long - 1, 1), SUBS, out_width, piece), BF16),
        vmem((max(n_short - 1, 1), SUBS, out_width, piece), BF16),
        vmem((n_long, SUBS, out_width, piece), BF16),
        vmem((max(n_short, 1), SUBS, out_width, piece), BF16),
        dma((n_long, SUBS)), dma((n_long, SUBS)),
        dma((max(n_short, 1), SUBS)), dma((max(n_short, 1), SUBS)),
    ]
    return pl.pallas_call(
        functools.partial(kernel, sizes),
        out_shape=jax.ShapeDtypeStruct((out_width, length), BF16),
        in_specs=[pl.BlockSpec(memory_space=pl.ANY)] * 9,
        out_specs=pl.BlockSpec(memory_space=pltpu.VMEM),
        scratch_shapes=scratch,
        compiler_params=pltpu.CompilerParams(
            collective_id=0, has_side_effects=True, vmem_limit_bytes=60 * 1024 * 1024
        ),
        name="layer",
    )(
        head_input, bc_input, conv_x, conv_bc, log_decay, d_skip, gate_z,
        norm_gain, w_out,
    ).T


def solution(mesh):
    n_ctx, nz = mesh.devices.shape
    sizes = (8, 4, 2, nz) if n_ctx == 64 else (2, max(n_ctx // 4, 1), 2, nz)
    split = Mesh(mesh.devices.reshape(sizes), ("y", "x", "c", "z"))
    return jax.shard_map(
        functools.partial(shards, sizes),
        mesh=split,
        in_specs=(
            P(CTX, "z"), P(CTX, None), P(None, "z"), P(), P("z", CTX), P("z"), P(CTX, "z"),
            P("z"), P("z", None),
        ),
        out_specs=P(CTX, "z"),
        check_vma=False,
    )
```

```python
import functools

import jax
import jax.numpy as jnp
from jax import lax
from jax.experimental import pallas as pl
from jax.experimental.pallas import tpu as pltpu
from jax.sharding import Mesh
from jax.sharding import PartitionSpec as P

F32 = jnp.float32
BF16 = jnp.bfloat16
MESH = pl.DeviceIdType.MESH
N = 128
K = 4
LANES = 128
ROWS = 64
SUBS = 4
CTX = ("y", "x", "c")


def split_three(value):
    high = value.astype(BF16)
    rest = value - high.astype(F32)
    middle = rest.astype(BF16)
    low = (rest - middle.astype(F32)).astype(BF16)
    return high, middle, low


def silu(value):
    half = 0.5 * value
    return half + half * jnp.tanh(half)


def dot(a, b, dims):
    return lax.dot_general(a, b, (dims, ((), ())), preferred_element_type=F32)


def iota(shape, dim):
    return lax.broadcasted_iota(jnp.int32, shape, dim)


def remote(source, target, send_sem, recv_sem, device):
    return pltpu.make_async_remote_copy(
        src_ref=source,
        dst_ref=target,
        send_sem=send_sem,
        recv_sem=recv_sem,
        device_id=device,
        device_id_type=MESH,
    )


def kernel(
    sizes,
    x_hbm, bc_hbm, cx_hbm, cbc_hbm, ld_hbm, d_hbm, gate_hbm, gain_hbm, w_hbm,
    out_ref,
    x_in, bc_in, cx, cbc, ld, d_skip, gate, gain, w,
    load_sem,
    halo_x, halo_bc, halo_send, halo_recv,
    xc, bcc, crow, cum, cum2, gram, scaled, later, state,
    decay_row, decay_send, decay_recv,
    total_row, total_send, total_recv,
    row_buf, row_send, row_recv, prefix,
    y_buf, y_send, y_recv,
    c_out, carried, c_send, c_recv,
    ya, yb, sq_part,
    sq_buf, sq_send, sq_recv,
    wt, ut, chunks, long_out, short_out, long_in, short_in,
    long_send, long_recv, short_send, short_recv,
):
    ny, nx, nc, nz = sizes
    nj = nx * nc
    y, x, c, z = (lax.axis_index(name) for name in ("y", "x", "c", "z"))
    j = x * nc + c
    flat = y * nj + j
    slab = N // nj
    heads, length = ld.shape
    width = x_in.shape[1]
    pairs = width // LANES
    cut = (pairs + 1) // 2 * LANES
    halves = [slice(0, cut), slice(cut, width)]
    row_steps = sorted(range(1, nj), key=lambda k: -min(k, nj - k))
    y_steps = sorted(range(1, ny), key=lambda k: -min(k, ny - k))

    loads = [
        pltpu.make_async_copy(source, target, load_sem.at[i])
        for i, (source, target) in enumerate(
            [
                (ld_hbm, ld), (x_hbm, x_in), (bc_hbm, bc_in), (cx_hbm, cx), (cbc_hbm, cbc),
                (d_hbm, d_skip), (gate_hbm, gate), (gain_hbm, gain), (w_hbm, w),
            ]
        )
    ]
    for load in loads:
        load.start()

    def member(index):
        return {"x": lax.div(index, nc), "c": lax.rem(index, nc)}

    def at(index):
        return {"y": lax.div(index, nj), **member(lax.rem(index, nj))}

    after = at(lax.rem(flat + 1, ny * nj))
    ahead = at(lax.rem(flat + ny * nj - 1, ny * nj))

    barrier = pltpu.get_barrier_semaphore()

    def greet(device):
        pl.semaphore_signal(barrier, inc=1, device_id=device, device_id_type=MESH)

    greet(after)
    greet(ahead)
    for k in range(1, ny):
        greet({"y": lax.rem(y + k, ny)})
    for k in range(1, nz):
        greet({"z": lax.rem(z + k, nz)})
    for k in range(1, nj):
        greet(member(lax.rem(j + k, nj)))

    pl.semaphore_wait(barrier, 2 + (ny - 1) + (nz - 1) + (nj - 1))
    tail = pl.ds(length - 16, 16)
    halos = [
        remote(x_hbm.at[tail], halo_x, halo_send.at[0], halo_recv.at[0], after),
        remote(bc_hbm.at[tail], halo_bc, halo_send.at[1], halo_recv.at[1], after),
    ]

    @pl.when(flat < ny * nj - 1)
    def _():
        for copy in halos:
            copy.start()

    loads[0].wait()
    padded = jnp.concatenate([ld[...], jnp.zeros((16 - heads, length), F32)], axis=0)
    upper = (iota((length, length), 0) <= iota((length, length), 1)).astype(BF16)
    three = dot(jnp.concatenate(split_three(padded), axis=0), upper, ((1,), (0,)))
    rows = three[0:16] + (three[16:32] + three[32:48])
    stacked = jnp.concatenate(split_three(rows), axis=0)
    pick = (iota((48, width), 0) & 15) == lax.shift_right_logical(iota((48, width), 1), 6)
    cum[...] = dot(stacked, pick.astype(BF16), ((0,), (0,)))
    decay_row[j] = cum[length - 1 : length, :]

    decays = []
    for k in range(1, nj):
        other = lax.rem(j + k, nj)
        copy = remote(
            decay_row.at[j], decay_row.at[j], decay_send.at[k], decay_recv.at[j], member(other)
        )
        copy.start()
        decays.append(copy)

    for load in loads[1:5]:
        load.wait()

    def filtered(block, taps):
        total = taps[K - 1 : K, :] * block[16:]
        for tap in range(K - 1):
            total = total + taps[tap : tap + 1, :] * pltpu.roll(block, K - 1 - tap, 0)[16:]
        return silu(total).astype(BF16)

    def convolve(here, block_x, block_bc):
        conv = filtered(block_x.astype(F32), cx)
        xc[here, :] = conv
        bcc[here, :] = filtered(block_bc.astype(F32), cbc)
        weight = jnp.exp(cum[length - 1 : length, :] - cum[here, :])
        scaled[here, :] = (conv.astype(F32) * weight).astype(BF16)

    def convolve_at(i, _):
        r = pl.multiple_of(i * ROWS, ROWS)
        block = pl.ds(pl.multiple_of(r - 16, 16), ROWS + 16)
        convolve(pl.ds(r, ROWS), x_in[block, :], bc_in[block, :])
        return 0

    lax.fori_loop(1, length // ROWS, convolve_at, 0)
    later[...] = dot(bcc[ROWS:length, 0:N], scaled[ROWS:length, :], ((0,), (0,)))

    @pl.when(flat == 0)
    def _():
        halo_x[...] = jnp.zeros((16, width), BF16)
        halo_bc[...] = jnp.zeros((16, 2 * N), BF16)

    @pl.when(flat > 0)
    def _():
        for copy in halos:
            copy.wait_recv()

    convolve(
        slice(0, ROWS),
        jnp.concatenate([halo_x[...], x_in[0:ROWS, :]], axis=0),
        jnp.concatenate([halo_bc[...], bc_in[0:ROWS, :]], axis=0),
    )

    def slice_of(index):
        return pl.ds(pl.multiple_of(index * slab, slab), slab)

    sent = []
    for half, lanes in enumerate(halves):
        first = dot(bcc[0:ROWS, 0:N], scaled[0:ROWS, lanes], ((0,), (0,)))
        state[:, lanes] = (later[:, lanes] + first).astype(BF16)
        for k in row_steps:
            other = lax.rem(j + k, nj)
            copy = remote(
                state.at[slice_of(other), lanes],
                row_buf.at[j, :, lanes],
                row_send.at[half, k],
                row_recv.at[half, j],
                member(other),
            )
            copy.start()
            sent.append(copy)
        row_buf[j, :, lanes] = state[slice_of(j), lanes]

    for k in range(1, nj):
        other = lax.rem(j + k, nj)
        remote(
            decay_row.at[other], decay_row.at[other], decay_send.at[k], decay_recv.at[other],
            member(other),
        ).wait_recv()
    whole = decay_row[0]
    for i in range(1, nj):
        whole = whole + decay_row[i]
    total_row[y] = whole
    totals = []
    for k in range(1, ny):
        copy = remote(
            total_row.at[y], total_row.at[y], total_send.at[k], total_recv.at[y],
            {"y": lax.rem(y + k, ny)},
        )
        copy.start()
        totals.append(copy)

    for h in range(heads):
        crow[h] = rows[h : h + 1]
    wide = heads * LANES
    pick2 = (iota((48, wide), 0) & 15) == lax.shift_right_logical(iota((48, wide), 1), 7)
    cum2[...] = dot(stacked, pick2.astype(BF16), ((0,), (0,)))
    gram[...] = dot(bcc[:, N : 2 * N], bcc[:, 0:N], ((1,), (1,)))
    left = iota((LANES, LANES), 1) < 64
    causal = iota((LANES, LANES), 0) >= iota((LANES, LANES), 1)
    loads[5].wait()

    def local_pair(i, _):
        lanes = pl.ds(pl.multiple_of(i * LANES, LANES), LANES)
        for block in range(length // LANES):
            t = slice(block * LANES, (block + 1) * LANES)
            results = []
            for side in range(2):
                h = 2 * i + side
                here = cum2[t, pl.ds(pl.multiple_of(h * LANES, LANES), LANES)]
                parts = []
                for other in range(block + 1):
                    s = slice(other * LANES, (other + 1) * LANES)
                    spread = here - crow[h, :, s]
                    if other == block:
                        part = jnp.where(causal, gram[t, s] * jnp.exp(jnp.minimum(spread, 0.0)), 0.0)
                    else:
                        part = gram[t, s] * jnp.exp(spread)
                    parts.append(part.astype(BF16))
                mixing = parts[0] if block == 0 else jnp.concatenate(parts, axis=1)
                results.append(dot(mixing, xc[0 : (block + 1) * LANES, lanes], ((1,), (0,))))
            skip = jnp.where(left, d_skip[2 * i], d_skip[2 * i + 1])
            ya[t, lanes] = jnp.where(left, results[0], results[1]) + skip * xc[t, lanes].astype(F32)
        return 0

    lax.fori_loop(0, 2, local_pair, 0)

    def y_copy(half, k):
        lanes = halves[half]
        return remote(
            y_buf.at[y, :, lanes], y_buf.at[y, :, lanes], y_send.at[half, k], y_recv.at[half, y],
            {"y": lax.rem(y + k, ny)},
        )

    for half, lanes in enumerate(halves):
        for k in row_steps:
            other = lax.rem(j + k, nj)
            theirs = row_buf.at[other, :, lanes]
            remote(
                theirs, theirs, row_send.at[half, k], row_recv.at[half, other], member(other)
            ).wait_recv()
        running = jnp.zeros((slab, lanes.stop - lanes.start), F32)
        for i in range(nj):
            prefix[i, :, lanes] = running
            running = jnp.exp(decay_row[i, :, lanes]) * running
            running = running + row_buf[i, :, lanes].astype(F32)
        y_buf[y, :, lanes] = running.astype(BF16)
        for k in y_steps:

            @pl.when(y + k < ny)
            def _(half=half, k=k):
                y_copy(half, k).start()

    lax.fori_loop(2, pairs, local_pair, 0)

    loads[6].wait()

    def gates(i, _):
        here = pl.ds(pl.multiple_of(i * ROWS, ROWS), ROWS)
        factor = silu(gate[here, :].astype(F32))
        ya[here, :] = ya[here, :] * factor
        yb[here, :] = jnp.exp(cum[here, :]) * factor
        return 0

    lax.fori_loop(0, length // ROWS, gates, 0)

    loads[8].wait()

    def turn(i, _):
        here = pl.ds(pl.multiple_of(i * LANES, LANES), LANES)
        wt[here, :] = w[:, here].T
        return 0

    blocks = w.shape[1] // LANES
    lax.fori_loop(0, blocks * 5 // 8, turn, 0)

    for k in range(1, ny):
        other = lax.rem(y + k, ny)
        remote(
            total_row.at[other], total_row.at[other], total_send.at[k], total_recv.at[other],
            {"y": other},
        ).wait_recv()
    returned = []
    for half, lanes in enumerate(halves):
        for k in y_steps:

            @pl.when(y >= k)
            def _(half=half, lanes=lanes, k=k):
                other = lax.rem(y - k + ny, ny)
                theirs = y_buf.at[other, :, lanes]
                remote(
                    theirs, theirs, y_send.at[half, k], y_recv.at[half, other], {"y": other}
                ).wait_recv()

        def earlier(i, total, lanes=lanes):
            return jnp.exp(total_row[i, :, lanes]) * total + y_buf[i, :, lanes].astype(F32)

        part_width = lanes.stop - lanes.start
        base = lax.fori_loop(0, y, earlier, jnp.zeros((slab, part_width), F32))
        fade = jnp.zeros((1, part_width), F32)
        for i in range(nj):
            c_out[i, :, lanes] = (jnp.exp(fade) * base + prefix[i, :, lanes]).astype(BF16)
            fade = fade + decay_row[i, :, lanes]
        for k in row_steps:
            other = lax.rem(j + k, nj)
            copy = remote(
                c_out.at[other, :, lanes], carried.at[slice_of(j), lanes], c_send.at[half, k],
                c_recv.at[half, j], member(other),
            )
            copy.start()
            returned.append(copy)
        carried[slice_of(j), lanes] = c_out[j, :, lanes]

    loads[7].wait()
    lax.fori_loop(blocks * 5 // 8, blocks, turn, 0)
    amount = gain[...].reshape(1, width)

    def await_carried(half):
        for k in row_steps:
            other = lax.rem(j + k, nj)
            theirs = carried.at[slice_of(other), halves[half]]
            remote(
                theirs, theirs, c_send.at[half, k], c_recv.at[half, other], member(other)
            ).wait_recv()

    def finish(half, here):
        lanes = halves[half]
        from_state = dot(bcc[here, N : 2 * N], carried[:, lanes], ((1,), (0,)))
        gated = ya[here, lanes] + yb[here, lanes] * from_state
        ut[lanes, here] = (gated * amount[:, lanes]).astype(BF16).T
        square = gated * gated
        total = square[:, 0:LANES]
        for begin in range(LANES, lanes.stop - lanes.start, LANES):
            total = total + square[:, begin : begin + LANES]
        sq_part[here, :] = total if half == 0 else sq_part[here, :] + total

    def finish_first(i, _):
        finish(0, pl.ds(pl.multiple_of(i * LANES, LANES), LANES))
        return 0

    await_carried(0)
    lax.fori_loop(0, length // LANES, finish_first, 0)

    rows_out = out_ref.shape[0]
    piece = length // SUBS

    def tokens(q):
        return pl.ds(pl.multiple_of(q * piece, piece), piece)

    def project_piece(d, q):
        here = pl.ds(pl.multiple_of(d * rows_out, 64), rows_out)
        chunks[d, q] = dot(wt[here, :], ut[:, tokens(q)], ((1,), (0,))).astype(BF16)

    def project(d):
        here = pl.ds(pl.multiple_of(d * rows_out, 64), rows_out)
        part = dot(wt[here, :], ut[...], ((1,), (0,))).astype(BF16)
        for q in range(SUBS):
            chunks[d, q] = part[:, q * piece : (q + 1) * piece]

    sign = 1 - 2 * c
    n_long = nz // 2
    n_short = n_long - 1

    def towards(offset):
        return lax.rem(z + offset * sign + 2 * nz, nz)

    def long_copy(source, step, q):
        return remote(
            source, long_in.at[step, q], long_send.at[step, q], long_recv.at[step, q],
            {"z": towards(1)},
        )

    def short_copy(source, step, q):
        return remote(
            source, short_in.at[step, q], short_send.at[step, q], short_recv.at[step, q],
            {"z": towards(-1)},
        )

    def begin(q, _):
        finish(1, tokens(q))
        project_piece(towards(n_long), q)
        long_copy(chunks.at[towards(n_long), q], 0, q).start()
        if n_short:
            project_piece(towards(-n_short), q)
            short_copy(chunks.at[towards(-n_short), q], 0, q).start()
        return 0

    await_carried(1)
    lax.fori_loop(0, SUBS, begin, 0)

    squares = jnp.zeros((16, length), F32)
    for term in split_three(sq_part[...]):
        squares = squares + dot(jnp.ones((16, LANES), BF16), term, ((1,), (1,)))
    sq_buf[z] = squares[0:1, :]
    shared = []
    for k in range(1, nz):
        copy = remote(
            sq_buf.at[z], sq_buf.at[z], sq_send.at[k], sq_recv.at[z], {"z": lax.rem(z + k, nz)}
        )
        copy.start()
        shared.append(copy)

    for step in range(1, n_long):
        project(towards(n_long - step))
        if step < n_short:
            project(towards(step - n_short))
    project(z)

    for step in range(1, n_long):

        def relay(q, _, step=step):
            long_copy(long_in.at[step - 1, q], step - 1, q).wait_recv()
            long_out[step - 1, q] = (
                long_in[step - 1, q].astype(F32) + chunks[towards(n_long - step), q].astype(F32)
            ).astype(BF16)
            long_copy(long_out.at[step - 1, q], step, q).start()
            if step < n_short:
                short_copy(short_in.at[step - 1, q], step - 1, q).wait_recv()
                short_out[step - 1, q] = (
                    short_in[step - 1, q].astype(F32)
                    + chunks[towards(step - n_short), q].astype(F32)
                ).astype(BF16)
                short_copy(short_out.at[step - 1, q], step, q).start()
            return 0

        lax.fori_loop(0, SUBS, relay, 0)

    for k in range(1, nz):
        other = lax.rem(z + k, nz)
        remote(sq_buf.at[other], sq_buf.at[other], sq_send.at[k], sq_recv.at[other], {"z": other}).wait_recv()
    def deliver(q, _):
        long_copy(long_in.at[n_long - 1, q], n_long - 1, q).wait_recv()
        total = chunks[z, q].astype(F32) + long_in[n_long - 1, q].astype(F32)
        if n_short:
            short_copy(short_in.at[n_short - 1, q], n_short - 1, q).wait_recv()
            total = total + short_in[n_short - 1, q].astype(F32)
        summed = sq_buf[0, :, tokens(q)]
        for i in range(1, nz):
            summed = summed + sq_buf[i, :, tokens(q)]
        scale = lax.rsqrt(summed * (1.0 / (width * nz)) + 1e-5)
        out_ref[:, tokens(q)] = (total * scale).astype(BF16)
        return 0

    lax.fori_loop(0, SUBS, deliver, 0)

    @pl.when(flat < ny * nj - 1)
    def _():
        for copy in halos:
            copy.wait_send()

    for copy in decays + totals + sent + returned + shared:
        copy.wait_send()
    for half in range(2):
        for k in y_steps:

            @pl.when(y + k < ny)
            def _(half=half, k=k):
                y_copy(half, k).wait_send()

    def drained(q, _):
        for step in range(n_long):
            long_copy(long_in.at[step, q], step, q).wait_send()
        for step in range(n_short):
            short_copy(short_in.at[step, q], step, q).wait_send()
        return 0

    lax.fori_loop(0, SUBS, drained, 0)


def shards(sizes, head_input, bc_input, conv_x, conv_bc, log_decay, d_skip, gate_z, norm_gain, w_out):
    ny, nx, nc, nz = sizes
    nj = nx * nc
    length, width = head_input.shape
    heads = log_decay.shape[0]
    slab = N // nj
    out_width = w_out.shape[1] // nz
    piece = length // SUBS
    n_long = nz // 2
    n_short = n_long - 1
    dma = pltpu.SemaphoreType.DMA
    vmem = pltpu.VMEM
    scratch = [
        vmem((length, width), BF16), vmem((length, 2 * N), BF16),
        vmem((K, width), F32), vmem((K, 2 * N), F32), vmem((heads, length), F32),
        pltpu.SMEM((heads,), F32), vmem((length, width), BF16), vmem((width,), F32),
        vmem(w_out.shape, BF16),
        dma((9,)),
        vmem((16, width), BF16), vmem((16, 2 * N), BF16), dma((2,)), dma((2,)),
        vmem((length, width), BF16), vmem((length, 2 * N), BF16),
        vmem((heads, 1, length), F32), vmem((length, width), F32), vmem((length, heads * LANES), F32),
        vmem((length, length), F32), vmem((length, width), BF16),
        vmem((N, width), F32), vmem((N, width), BF16),
        vmem((nj, 1, width), F32), dma((nj,)), dma((nj,)),
        vmem((ny, 1, width), F32), dma((ny,)), dma((ny,)),
        vmem((nj, slab, width), BF16), dma((2, nj)), dma((2, nj)), vmem((nj, slab, width), F32),
        vmem((ny, slab, width), BF16), dma((2, ny)), dma((2, ny)),
        vmem((nj, slab, width), BF16), vmem((N, width), BF16), dma((2, nj)), dma((2, nj)),
        vmem((length, width), F32), vmem((length, width), F32), vmem((length, LANES), F32),
        vmem((nz, 1, length), F32), dma((nz,)), dma((nz,)),
        vmem(w_out.shape[::-1], BF16), vmem((width, length), BF16),
        vmem((nz, SUBS, out_width, piece), BF16),
        vmem((max(n_long - 1, 1), SUBS, out_width, piece), BF16),
        vmem((max(n_short - 1, 1), SUBS, out_width, piece), BF16),
        vmem((n_long, SUBS, out_width, piece), BF16),
        vmem((max(n_short, 1), SUBS, out_width, piece), BF16),
        dma((n_long, SUBS)), dma((n_long, SUBS)),
        dma((max(n_short, 1), SUBS)), dma((max(n_short, 1), SUBS)),
    ]
    return pl.pallas_call(
        functools.partial(kernel, sizes),
        out_shape=pltpu.VMEM((out_width, length), BF16),
        in_specs=[pl.BlockSpec(memory_space=pl.ANY)] * 9,
        out_specs=pl.BlockSpec(memory_space=pltpu.VMEM),
        scratch_shapes=scratch,
        compiler_params=pltpu.CompilerParams(
            collective_id=0, has_side_effects=True, vmem_limit_bytes=60 * 1024 * 1024
        ),
        name="layer",
    )(
        head_input, bc_input, conv_x, conv_bc, log_decay, d_skip, gate_z,
        norm_gain, w_out,
    ).T


def solution(mesh):
    n_ctx, nz = mesh.devices.shape
    sizes = (8, 4, 2, nz) if n_ctx == 64 else (2, max(n_ctx // 4, 1), 2, nz)
    split = Mesh(mesh.devices.reshape(sizes), ("y", "x", "c", "z"))
    return jax.shard_map(
        functools.partial(shards, sizes),
        mesh=split,
        in_specs=(
            P(CTX, "z"), P(CTX, None), P(None, "z"), P(), P("z", CTX), P("z"), P(CTX, "z"),
            P("z"), P("z", None),
        ),
        out_specs=P(CTX, "z"),
        check_vma=False,
    )
```

```python
import functools

import jax
import jax.numpy as jnp
from jax import lax
from jax.experimental import pallas as pl
from jax.experimental.pallas import tpu as pltpu
from jax.sharding import Mesh
from jax.sharding import PartitionSpec as P

F32 = jnp.float32
BF16 = jnp.bfloat16
MESH = pl.DeviceIdType.MESH
N = 128
K = 4
LANES = 128
ROWS = 64
SUBS = 4
CTX = ("y", "x", "c")


def split_three(value):
    high = value.astype(BF16)
    rest = value - high.astype(F32)
    middle = rest.astype(BF16)
    low = (rest - middle.astype(F32)).astype(BF16)
    return high, middle, low


def silu(value):
    half = 0.5 * value
    return half + half * jnp.tanh(half)


def dot(a, b, dims):
    return lax.dot_general(a, b, (dims, ((), ())), preferred_element_type=F32)


def iota(shape, dim):
    return lax.broadcasted_iota(jnp.int32, shape, dim)


def remote(source, target, send_sem, recv_sem, device):
    return pltpu.make_async_remote_copy(
        src_ref=source,
        dst_ref=target,
        send_sem=send_sem,
        recv_sem=recv_sem,
        device_id=device,
        device_id_type=MESH,
    )


def kernel(
    sizes,
    x_hbm, bc_hbm, cx_hbm, cbc_hbm, ld_hbm, d_hbm, gate_hbm, gain_hbm, w_hbm,
    out_ref,
    x_in, bc_in, cx, cbc, ld, d_skip, gate, gain, w,
    load_sem,
    halo_x, halo_bc, halo_send, halo_recv,
    xc, bcc, crow, cum, cum2, gram, scaled, later, state,
    decay_row, decay_send, decay_recv,
    total_row, total_send, total_recv,
    row_buf, row_send, row_recv, prefix,
    y_buf, y_send, y_recv,
    c_out, carried, c_send, c_recv,
    ya, yb, sq_part,
    sq_buf, sq_send, sq_recv,
    wt, ut, chunks, long_out, short_out, long_in, short_in,
    long_send, long_recv, short_send, short_recv,
):
    ny, nx, nc, nz = sizes
    nj = nx * nc
    y, x, c, z = (lax.axis_index(name) for name in ("y", "x", "c", "z"))
    j = x * nc + c
    flat = y * nj + j
    slab = N // nj
    heads, length = ld.shape
    width = x_in.shape[1]
    pairs = width // LANES
    cut = (pairs + 1) // 2 * LANES
    halves = [slice(0, cut), slice(cut, width)]
    row_steps = sorted(range(1, nj), key=lambda k: -min(k, nj - k))
    y_steps = sorted(range(1, ny), key=lambda k: -min(k, ny - k))

    def member(index):
        return {"x": lax.div(index, nc), "c": lax.rem(index, nc)}

    def at(index):
        return {"y": lax.div(index, nj), **member(lax.rem(index, nj))}

    after = at(lax.rem(flat + 1, ny * nj))
    ahead = at(lax.rem(flat + ny * nj - 1, ny * nj))

    barrier = pltpu.get_barrier_semaphore()

    def greet(device):
        pl.semaphore_signal(barrier, inc=1, device_id=device, device_id_type=MESH)

    for k in y_steps:
        greet({"y": lax.rem(y + k, ny)})
    greet(after)
    greet(ahead)
    for k in row_steps:
        greet(member(lax.rem(j + k, nj)))
    for k in range(1, nz):
        greet({"z": lax.rem(z + k, nz)})

    loads = [
        pltpu.make_async_copy(source, target, load_sem.at[i])
        for i, (source, target) in enumerate(
            [
                (ld_hbm, ld), (x_hbm, x_in), (bc_hbm, bc_in), (cx_hbm, cx), (cbc_hbm, cbc),
                (d_hbm, d_skip), (gate_hbm, gate), (gain_hbm, gain), (w_hbm, w),
            ]
        )
    ]
    for load in loads:
        load.start()

    loads[1].wait()
    loads[2].wait()
    pl.semaphore_wait(barrier, 2 + (ny - 1) + (nz - 1) + (nj - 1))
    tail = pl.ds(length - 16, 16)
    halos = [
        remote(x_in.at[tail], halo_x, halo_send.at[0], halo_recv.at[0], after),
        remote(bc_in.at[tail], halo_bc, halo_send.at[1], halo_recv.at[1], after),
    ]

    @pl.when(flat < ny * nj - 1)
    def _():
        for copy in halos:
            copy.start()

    loads[0].wait()
    padded = jnp.concatenate([ld[...], jnp.zeros((16 - heads, length), F32)], axis=0)
    upper = (iota((length, length), 0) <= iota((length, length), 1)).astype(BF16)
    three = dot(jnp.concatenate(split_three(padded), axis=0), upper, ((1,), (0,)))
    rows = three[0:16] + (three[16:32] + three[32:48])
    stacked = jnp.concatenate(split_three(rows), axis=0)
    pick = (iota((48, width), 0) & 15) == lax.shift_right_logical(iota((48, width), 1), 6)
    cum[...] = dot(stacked, pick.astype(BF16), ((0,), (0,)))
    decay_row[j] = cum[length - 1 : length, :]

    decays = []
    for k in range(1, nj):
        other = lax.rem(j + k, nj)
        copy = remote(
            decay_row.at[j], decay_row.at[j], decay_send.at[k], decay_recv.at[j], member(other)
        )
        copy.start()
        decays.append(copy)

    loads[3].wait()
    loads[4].wait()

    def filtered(block, taps):
        total = taps[K - 1 : K, :] * block[16:]
        for tap in range(K - 1):
            total = total + taps[tap : tap + 1, :] * pltpu.roll(block, K - 1 - tap, 0)[16:]
        return silu(total).astype(BF16)

    def convolve(here, lanes, block_x):
        conv = filtered(block_x.astype(F32), cx.at[:, lanes])
        xc[here, lanes] = conv
        weight = jnp.exp(cum[length - 1 : length, lanes] - cum[here, lanes])
        scaled[here, lanes] = (conv.astype(F32) * weight).astype(BF16)

    def convolve_at(i, _):
        r = pl.multiple_of(i * ROWS, ROWS)
        block = pl.ds(pl.multiple_of(r - 16, 16), ROWS + 16)
        convolve(pl.ds(r, ROWS), slice(0, width), x_in[block, :])
        bcc[pl.ds(r, ROWS), :] = filtered(bc_in[block, :].astype(F32), cbc)
        return 0

    lax.fori_loop(1, length // ROWS, convolve_at, 0)
    later[...] = dot(bcc[ROWS:length, 0:N], scaled[ROWS:length, :], ((0,), (0,)))

    @pl.when(flat == 0)
    def _():
        halo_x[...] = jnp.zeros((16, width), BF16)
        halo_bc[...] = jnp.zeros((16, 2 * N), BF16)

    @pl.when(flat > 0)
    def _():
        for copy in halos:
            copy.wait_recv()

    begun = slice(0, ROWS)
    block_bc = jnp.concatenate([halo_bc[...], bc_in[begun, :]], axis=0)
    bcc[begun, :] = filtered(block_bc.astype(F32), cbc)

    def slice_of(index):
        return pl.ds(pl.multiple_of(index * slab, slab), slab)

    sent = []
    for half, lanes in enumerate(halves):
        convolve(
            begun, lanes, jnp.concatenate([halo_x[:, lanes], x_in[begun, lanes]], axis=0)
        )
        first = dot(bcc[begun, 0:N], scaled[begun, lanes], ((0,), (0,)))
        state[:, lanes] = (later[:, lanes] + first).astype(BF16)
        for k in row_steps:
            other = lax.rem(j + k, nj)
            copy = remote(
                state.at[slice_of(other), lanes],
                row_buf.at[j, :, lanes],
                row_send.at[half, k],
                row_recv.at[half, j],
                member(other),
            )
            copy.start()
            sent.append(copy)
        row_buf[j, :, lanes] = state[slice_of(j), lanes]

    for k in range(1, nj):
        other = lax.rem(j + k, nj)
        remote(
            decay_row.at[other], decay_row.at[other], decay_send.at[k], decay_recv.at[other],
            member(other),
        ).wait_recv()
    whole = decay_row[0]
    for i in range(1, nj):
        whole = whole + decay_row[i]
    total_row[y] = whole
    totals = []
    for k in range(1, ny):
        copy = remote(
            total_row.at[y], total_row.at[y], total_send.at[k], total_recv.at[y],
            {"y": lax.rem(y + k, ny)},
        )
        copy.start()
        totals.append(copy)

    for h in range(heads):
        crow[h] = rows[h : h + 1]
    wide = heads * LANES
    pick2 = (iota((48, wide), 0) & 15) == lax.shift_right_logical(iota((48, wide), 1), 7)
    cum2[...] = dot(stacked, pick2.astype(BF16), ((0,), (0,)))
    gram[...] = dot(bcc[:, N : 2 * N], bcc[:, 0:N], ((1,), (1,)))
    left = iota((LANES, LANES), 1) < 64
    causal = iota((LANES, LANES), 0) >= iota((LANES, LANES), 1)
    loads[5].wait()

    def local_pair(i, _):
        lanes = pl.ds(pl.multiple_of(i * LANES, LANES), LANES)
        for block in range(length // LANES):
            t = slice(block * LANES, (block + 1) * LANES)
            results = []
            for side in range(2):
                h = 2 * i + side
                here = cum2[t, pl.ds(pl.multiple_of(h * LANES, LANES), LANES)]
                parts = []
                for other in range(block + 1):
                    s = slice(other * LANES, (other + 1) * LANES)
                    spread = here - crow[h, :, s]
                    if other == block:
                        part = jnp.where(causal, gram[t, s] * jnp.exp(jnp.minimum(spread, 0.0)), 0.0)
                    else:
                        part = gram[t, s] * jnp.exp(spread)
                    parts.append(part.astype(BF16))
                mixing = parts[0] if block == 0 else jnp.concatenate(parts, axis=1)
                results.append(dot(mixing, xc[0 : (block + 1) * LANES, lanes], ((1,), (0,))))
            skip = jnp.where(left, d_skip[2 * i], d_skip[2 * i + 1])
            ya[t, lanes] = jnp.where(left, results[0], results[1]) + skip * xc[t, lanes].astype(F32)
        return 0

    lax.fori_loop(0, 3, local_pair, 0)

    def y_copy(half, k):
        lanes = halves[half]
        return remote(
            y_buf.at[y, :, lanes], y_buf.at[y, :, lanes], y_send.at[half, k], y_recv.at[half, y],
            {"y": lax.rem(y + k, ny)},
        )

    for half, lanes in enumerate(halves):
        for k in row_steps:
            other = lax.rem(j + k, nj)
            theirs = row_buf.at[other, :, lanes]
            remote(
                theirs, theirs, row_send.at[half, k], row_recv.at[half, other], member(other)
            ).wait_recv()
        running = jnp.zeros((slab, lanes.stop - lanes.start), F32)
        for i in range(nj):
            prefix[i, :, lanes] = running
            running = jnp.exp(decay_row[i, :, lanes]) * running
            running = running + row_buf[i, :, lanes].astype(F32)
        y_buf[y, :, lanes] = running.astype(BF16)
        for k in y_steps:

            @pl.when(y + k < ny)
            def _(half=half, k=k):
                y_copy(half, k).start()

    n_blocks = length // ROWS
    pairs_first = jnp.where(y >= 3, pairs, 3)
    gates_first = jnp.where(y >= 3, n_blocks, 0)
    loads[6].wait()

    def gates(i, _):
        here = pl.ds(pl.multiple_of(i * ROWS, ROWS), ROWS)
        factor = silu(gate[here, :].astype(F32))
        ya[here, :] = ya[here, :] * factor
        yb[here, :] = jnp.exp(cum[here, :]) * factor
        return 0

    lax.fori_loop(3, pairs_first, local_pair, 0)
    lax.fori_loop(0, gates_first, gates, 0)

    for k in range(1, ny):
        other = lax.rem(y + k, ny)
        remote(
            total_row.at[other], total_row.at[other], total_send.at[k], total_recv.at[other],
            {"y": other},
        ).wait_recv()
    returned = []
    for half, lanes in enumerate(halves):
        for k in y_steps:

            @pl.when(y >= k)
            def _(half=half, lanes=lanes, k=k):
                other = lax.rem(y - k + ny, ny)
                theirs = y_buf.at[other, :, lanes]
                remote(
                    theirs, theirs, y_send.at[half, k], y_recv.at[half, other], {"y": other}
                ).wait_recv()

        def earlier(i, total, lanes=lanes):
            return jnp.exp(total_row[i, :, lanes]) * total + y_buf[i, :, lanes].astype(F32)

        part_width = lanes.stop - lanes.start
        base = lax.fori_loop(0, y, earlier, jnp.zeros((slab, part_width), F32))
        fade = jnp.zeros((1, part_width), F32)
        for i in range(nj):
            c_out[i, :, lanes] = (jnp.exp(fade) * base + prefix[i, :, lanes]).astype(BF16)
            fade = fade + decay_row[i, :, lanes]
        for k in row_steps:
            other = lax.rem(j + k, nj)
            copy = remote(
                c_out.at[other, :, lanes], carried.at[slice_of(j), lanes], c_send.at[half, k],
                c_recv.at[half, j], member(other),
            )
            copy.start()
            returned.append(copy)
        carried[slice_of(j), lanes] = c_out[j, :, lanes]

    lax.fori_loop(pairs_first, pairs, local_pair, 0)
    lax.fori_loop(gates_first, n_blocks, gates, 0)

    rows_out = out_ref.shape[0]
    sign = 1 - 2 * c
    n_long = nz // 2
    n_short = n_long - 1

    def towards(offset):
        return lax.rem(z + offset * sign + 2 * nz, nz)

    def turn(d):
        begin = lax.div(d * rows_out, LANES)

        def turn_block(i, _):
            here = pl.ds(pl.multiple_of((begin + i) * LANES, LANES), LANES)
            wt[here, :] = w[:, here].T
            return 0

        lax.fori_loop(0, pl.cdiv(rows_out, LANES), turn_block, 0)

    loads[8].wait()
    turn(towards(n_long))
    if n_short:
        turn(towards(-n_short))
    loads[7].wait()
    amount = gain[...].reshape(1, width)

    def await_carried(half):
        for k in row_steps:
            other = lax.rem(j + k, nj)
            theirs = carried.at[slice_of(other), halves[half]]
            remote(
                theirs, theirs, c_send.at[half, k], c_recv.at[half, other], member(other)
            ).wait_recv()

    def finish(half, here):
        lanes = halves[half]
        from_state = dot(bcc[here, N : 2 * N], carried[:, lanes], ((1,), (0,)))
        gated = ya[here, lanes] + yb[here, lanes] * from_state
        ut[lanes, here] = (gated * amount[:, lanes]).astype(BF16).T
        square = gated * gated
        total = square[:, 0:LANES]
        for begin in range(LANES, lanes.stop - lanes.start, LANES):
            total = total + square[:, begin : begin + LANES]
        sq_part[here, :] = total if half == 0 else sq_part[here, :] + total

    def finish_first(i, _):
        finish(0, pl.ds(pl.multiple_of(i * LANES, LANES), LANES))
        return 0

    await_carried(0)
    lax.fori_loop(0, length // LANES, finish_first, 0)

    piece = length // SUBS

    def tokens(q):
        return pl.ds(pl.multiple_of(q * piece, piece), piece)

    def project_piece(d, q):
        here = pl.ds(pl.multiple_of(d * rows_out, 64), rows_out)
        chunks[d, q] = dot(wt[here, :], ut[:, tokens(q)], ((1,), (0,))).astype(BF16)

    def project(d):
        here = pl.ds(pl.multiple_of(d * rows_out, 64), rows_out)
        part = dot(wt[here, :], ut[...], ((1,), (0,))).astype(BF16)
        for q in range(SUBS):
            chunks[d, q] = part[:, q * piece : (q + 1) * piece]

    def long_copy(source, step, q):
        return remote(
            source, long_in.at[step, q], long_send.at[step, q], long_recv.at[step, q],
            {"z": towards(1)},
        )

    def short_copy(source, step, q):
        return remote(
            source, short_in.at[step, q], short_send.at[step, q], short_recv.at[step, q],
            {"z": towards(-1)},
        )

    def begin(q, _):
        finish(1, tokens(q))
        project_piece(towards(n_long), q)
        long_copy(chunks.at[towards(n_long), q], 0, q).start()
        if n_short:
            project_piece(towards(-n_short), q)
            short_copy(chunks.at[towards(-n_short), q], 0, q).start()
        return 0

    await_carried(1)
    lax.fori_loop(0, SUBS, begin, 0)

    squares = jnp.zeros((16, length), F32)
    for term in split_three(sq_part[...]):
        squares = squares + dot(jnp.ones((16, LANES), BF16), term, ((1,), (1,)))
    sq_buf[z] = squares[0:1, :]
    shared = []
    for k in range(1, nz):
        copy = remote(
            sq_buf.at[z], sq_buf.at[z], sq_send.at[k], sq_recv.at[z], {"z": lax.rem(z + k, nz)}
        )
        copy.start()
        shared.append(copy)

    def turn_and_project(d):
        turn(d)
        project(d)

    if n_long == 1:
        turn_and_project(z)
    for step in range(1, n_long):
        turn_and_project(towards(n_long - step))
        if step < n_short:
            turn_and_project(towards(step - n_short))
        if step == n_long - 1:
            turn_and_project(z)

        def relay(q, _, step=step):
            long_copy(long_in.at[step - 1, q], step - 1, q).wait_recv()
            long_out[step - 1, q] = (
                long_in[step - 1, q].astype(F32) + chunks[towards(n_long - step), q].astype(F32)
            ).astype(BF16)
            long_copy(long_out.at[step - 1, q], step, q).start()
            if step < n_short:
                short_copy(short_in.at[step - 1, q], step - 1, q).wait_recv()
                short_out[step - 1, q] = (
                    short_in[step - 1, q].astype(F32)
                    + chunks[towards(step - n_short), q].astype(F32)
                ).astype(BF16)
                short_copy(short_out.at[step - 1, q], step, q).start()
            return 0

        lax.fori_loop(0, SUBS, relay, 0)

    for k in range(1, nz):
        other = lax.rem(z + k, nz)
        remote(sq_buf.at[other], sq_buf.at[other], sq_send.at[k], sq_recv.at[other], {"z": other}).wait_recv()
    def deliver(q, _):
        long_copy(long_in.at[n_long - 1, q], n_long - 1, q).wait_recv()
        total = chunks[z, q].astype(F32) + long_in[n_long - 1, q].astype(F32)
        if n_short:
            short_copy(short_in.at[n_short - 1, q], n_short - 1, q).wait_recv()
            total = total + short_in[n_short - 1, q].astype(F32)
        summed = sq_buf[0, :, tokens(q)]
        for i in range(1, nz):
            summed = summed + sq_buf[i, :, tokens(q)]
        scale = lax.rsqrt(summed * (1.0 / (width * nz)) + 1e-5)
        out_ref[:, tokens(q)] = (total * scale).astype(BF16)
        return 0

    lax.fori_loop(0, SUBS, deliver, 0)

    @pl.when(flat < ny * nj - 1)
    def _():
        for copy in halos:
            copy.wait_send()

    for copy in decays + totals + sent + returned + shared:
        copy.wait_send()
    for half in range(2):
        for k in y_steps:

            @pl.when(y + k < ny)
            def _(half=half, k=k):
                y_copy(half, k).wait_send()

    def drained(q, _):
        for step in range(n_long):
            long_copy(long_in.at[step, q], step, q).wait_send()
        for step in range(n_short):
            short_copy(short_in.at[step, q], step, q).wait_send()
        return 0

    lax.fori_loop(0, SUBS, drained, 0)


def shards(sizes, head_input, bc_input, conv_x, conv_bc, log_decay, d_skip, gate_z, norm_gain, w_out):
    ny, nx, nc, nz = sizes
    nj = nx * nc
    length, width = head_input.shape
    heads = log_decay.shape[0]
    slab = N // nj
    out_width = w_out.shape[1] // nz
    piece = length // SUBS
    n_long = nz // 2
    n_short = n_long - 1
    dma = pltpu.SemaphoreType.DMA
    vmem = pltpu.VMEM
    scratch = [
        vmem((length, width), BF16), vmem((length, 2 * N), BF16),
        vmem((K, width), F32), vmem((K, 2 * N), F32), vmem((heads, length), F32),
        pltpu.SMEM((heads,), F32), vmem((length, width), BF16), vmem((width,), F32),
        vmem(w_out.shape, BF16),
        dma((9,)),
        vmem((16, width), BF16), vmem((16, 2 * N), BF16), dma((2,)), dma((2,)),
        vmem((length, width), BF16), vmem((length, 2 * N), BF16),
        vmem((heads, 1, length), F32), vmem((length, width), F32), vmem((length, heads * LANES), F32),
        vmem((length, length), F32), vmem((length, width), BF16),
        vmem((N, width), F32), vmem((N, width), BF16),
        vmem((nj, 1, width), F32), dma((nj,)), dma((nj,)),
        vmem((ny, 1, width), F32), dma((ny,)), dma((ny,)),
        vmem((nj, slab, width), BF16), dma((2, nj)), dma((2, nj)), vmem((nj, slab, width), F32),
        vmem((ny, slab, width), BF16), dma((2, ny)), dma((2, ny)),
        vmem((nj, slab, width), BF16), vmem((N, width), BF16), dma((2, nj)), dma((2, nj)),
        vmem((length, width), F32), vmem((length, width), F32), vmem((length, LANES), F32),
        vmem((nz, 1, length), F32), dma((nz,)), dma((nz,)),
        vmem(w_out.shape[::-1], BF16), vmem((width, length), BF16),
        vmem((nz, SUBS, out_width, piece), BF16),
        vmem((max(n_long - 1, 1), SUBS, out_width, piece), BF16),
        vmem((max(n_short - 1, 1), SUBS, out_width, piece), BF16),
        vmem((n_long, SUBS, out_width, piece), BF16),
        vmem((max(n_short, 1), SUBS, out_width, piece), BF16),
        dma((n_long, SUBS)), dma((n_long, SUBS)),
        dma((max(n_short, 1), SUBS)), dma((max(n_short, 1), SUBS)),
    ]
    return pl.pallas_call(
        functools.partial(kernel, sizes),
        out_shape=pltpu.VMEM((out_width, length), BF16),
        in_specs=[pl.BlockSpec(memory_space=pl.ANY)] * 9,
        out_specs=pl.BlockSpec(memory_space=pltpu.VMEM),
        scratch_shapes=scratch,
        compiler_params=pltpu.CompilerParams(
            collective_id=0, has_side_effects=True, vmem_limit_bytes=60 * 1024 * 1024
        ),
        name="layer",
    )(
        head_input, bc_input, conv_x, conv_bc, log_decay, d_skip, gate_z,
        norm_gain, w_out,
    ).T


def solution(mesh):
    n_ctx, nz = mesh.devices.shape
    sizes = (8, 4, 2, nz) if n_ctx == 64 else (2, max(n_ctx // 4, 1), 2, nz)
    split = Mesh(mesh.devices.reshape(sizes), ("y", "x", "c", "z"))
    return jax.shard_map(
        functools.partial(shards, sizes),
        mesh=split,
        in_specs=(
            P(CTX, "z"), P(CTX, None), P(None, "z"), P(), P("z", CTX), P("z"), P(CTX, "z"),
            P("z"), P("z", None),
        ),
        out_specs=P(CTX, "z"),
        check_vma=False,
    )
```

```python
import functools

import jax
import jax.numpy as jnp
from jax import lax
from jax.experimental import pallas as pl
from jax.experimental.pallas import tpu as pltpu
from jax.sharding import Mesh
from jax.sharding import PartitionSpec as P

F32 = jnp.float32
BF16 = jnp.bfloat16
MESH = pl.DeviceIdType.MESH
N = 128
K = 4
LANES = 128
ROWS = 64
SUBS = 4
CTX = ("y", "x", "c")


def split_three(value):
    high = value.astype(BF16)
    rest = value - high.astype(F32)
    middle = rest.astype(BF16)
    low = (rest - middle.astype(F32)).astype(BF16)
    return high, middle, low


def silu(value):
    half = 0.5 * value
    return half + half * jnp.tanh(half)


def dot(a, b, dims):
    return lax.dot_general(a, b, (dims, ((), ())), preferred_element_type=F32)


def iota(shape, dim):
    return lax.broadcasted_iota(jnp.int32, shape, dim)


def remote(source, target, send_sem, recv_sem, device):
    return pltpu.make_async_remote_copy(
        src_ref=source,
        dst_ref=target,
        send_sem=send_sem,
        recv_sem=recv_sem,
        device_id=device,
        device_id_type=MESH,
    )


def kernel(
    sizes,
    x_hbm, bc_hbm, cx_hbm, cbc_hbm, ld_hbm, d_hbm, gate_hbm, gain_hbm, w_hbm,
    out_ref,
    x_in, bc_in, cx, cbc, ld, d_skip, gate, gain, w,
    load_sem,
    halo_x, halo_bc, halo_send, halo_recv,
    xc, bcc, crow, cum, cum2, gram, scaled, later, state,
    decay_row, decay_send, decay_recv,
    total_row, total_send, total_recv,
    row_buf, row_send, row_recv, prefix,
    y_buf, y_send, y_recv,
    c_out, carried, c_send, c_recv,
    ya, yb, sq_part,
    sq_buf, sq_send, sq_recv,
    wt, ut, chunks, long_out, short_out, long_in, short_in,
    long_send, long_recv, short_send, short_recv,
):
    ny, nx, nc, nz = sizes
    nj = nx * nc
    y, x, c, z = (lax.axis_index(name) for name in ("y", "x", "c", "z"))
    j = x * nc + c
    flat = y * nj + j
    slab = N // nj
    heads, length = ld.shape
    width = x_in.shape[1]
    pairs = width // LANES
    cut = pairs // 2 * LANES
    halves = [slice(0, cut), slice(cut, width)]
    row_steps = sorted(range(1, nj), key=lambda k: -min(k, nj - k))
    y_steps = sorted(range(1, ny), key=lambda k: -min(k, ny - k))

    def member(index):
        return {"x": lax.div(index, nc), "c": lax.rem(index, nc)}

    def at(index):
        return {"y": lax.div(index, nj), **member(lax.rem(index, nj))}

    after = at(lax.rem(flat + 1, ny * nj))
    ahead = at(lax.rem(flat + ny * nj - 1, ny * nj))

    barrier = pltpu.get_barrier_semaphore()

    def greet(device):
        pl.semaphore_signal(barrier, inc=1, device_id=device, device_id_type=MESH)

    for k in y_steps:
        greet({"y": lax.rem(y + k, ny)})
    greet(after)
    greet(ahead)
    for k in row_steps:
        greet(member(lax.rem(j + k, nj)))
    for k in range(1, nz):
        greet({"z": lax.rem(z + k, nz)})

    loads = [
        pltpu.make_async_copy(source, target, load_sem.at[i])
        for i, (source, target) in enumerate(
            [
                (ld_hbm, ld), (x_hbm, x_in), (bc_hbm, bc_in), (cx_hbm, cx), (cbc_hbm, cbc),
                (d_hbm, d_skip), (gate_hbm, gate), (gain_hbm, gain), (w_hbm, w),
            ]
        )
    ]
    for load in loads:
        load.start()

    loads[1].wait()
    loads[2].wait()
    pl.semaphore_wait(barrier, 2 + (ny - 1) + (nz - 1) + (nj - 1))
    tail = pl.ds(length - 16, 16)
    halos = [
        remote(x_in.at[tail], halo_x, halo_send.at[0], halo_recv.at[0], after),
        remote(bc_in.at[tail], halo_bc, halo_send.at[1], halo_recv.at[1], after),
    ]

    @pl.when(flat < ny * nj - 1)
    def _():
        for copy in halos:
            copy.start()

    loads[0].wait()
    padded = jnp.concatenate([ld[...], jnp.zeros((16 - heads, length), F32)], axis=0)
    upper = (iota((length, length), 0) <= iota((length, length), 1)).astype(BF16)
    three = dot(jnp.concatenate(split_three(padded), axis=0), upper, ((1,), (0,)))
    rows = three[0:16] + (three[16:32] + three[32:48])
    stacked = jnp.concatenate(split_three(rows), axis=0)
    pick = (iota((48, width), 0) & 15) == lax.shift_right_logical(iota((48, width), 1), 6)
    cum[...] = dot(stacked, pick.astype(BF16), ((0,), (0,)))
    decay_row[j] = cum[length - 1 : length, :]

    decays = []
    for k in range(1, nj):
        other = lax.rem(j + k, nj)
        copy = remote(
            decay_row.at[j], decay_row.at[j], decay_send.at[k], decay_recv.at[j], member(other)
        )
        copy.start()
        decays.append(copy)

    loads[3].wait()
    loads[4].wait()

    def filtered(block, taps):
        total = taps[K - 1 : K, :] * block[16:]
        for tap in range(K - 1):
            total = total + taps[tap : tap + 1, :] * pltpu.roll(block, K - 1 - tap, 0)[16:]
        return silu(total).astype(BF16)

    def convolve(here, lanes, block_x):
        conv = filtered(block_x.astype(F32), cx.at[:, lanes])
        xc[here, lanes] = conv
        weight = jnp.exp(cum[length - 1 : length, lanes] - cum[here, lanes])
        scaled[here, lanes] = (conv.astype(F32) * weight).astype(BF16)

    def convolve_at(i, _):
        r = pl.multiple_of(i * ROWS, ROWS)
        block = pl.ds(pl.multiple_of(r - 16, 16), ROWS + 16)
        convolve(pl.ds(r, ROWS), slice(0, width), x_in[block, :])
        bcc[pl.ds(r, ROWS), :] = filtered(bc_in[block, :].astype(F32), cbc)
        return 0

    lax.fori_loop(1, length // ROWS, convolve_at, 0)
    later[...] = dot(bcc[ROWS:length, 0:N], scaled[ROWS:length, :], ((0,), (0,)))

    @pl.when(flat == 0)
    def _():
        halo_x[...] = jnp.zeros((16, width), BF16)
        halo_bc[...] = jnp.zeros((16, 2 * N), BF16)

    @pl.when(flat > 0)
    def _():
        for copy in halos:
            copy.wait_recv()

    begun = slice(0, ROWS)
    block_bc = jnp.concatenate([halo_bc[...], bc_in[begun, :]], axis=0)
    bcc[begun, :] = filtered(block_bc.astype(F32), cbc)

    def slice_of(index):
        return pl.ds(pl.multiple_of(index * slab, slab), slab)

    sent = []
    for half, lanes in enumerate(halves):
        convolve(
            begun, lanes, jnp.concatenate([halo_x[:, lanes], x_in[begun, lanes]], axis=0)
        )
        first = dot(bcc[begun, 0:N], scaled[begun, lanes], ((0,), (0,)))
        state[:, lanes] = (later[:, lanes] + first).astype(BF16)
        for k in row_steps:
            other = lax.rem(j + k, nj)
            copy = remote(
                state.at[slice_of(other), lanes],
                row_buf.at[j, :, lanes],
                row_send.at[half, k],
                row_recv.at[half, j],
                member(other),
            )
            copy.start()
            sent.append(copy)
        row_buf[j, :, lanes] = state[slice_of(j), lanes]

    for k in range(1, nj):
        other = lax.rem(j + k, nj)
        remote(
            decay_row.at[other], decay_row.at[other], decay_send.at[k], decay_recv.at[other],
            member(other),
        ).wait_recv()
    whole = decay_row[0]
    for i in range(1, nj):
        whole = whole + decay_row[i]
    total_row[y] = whole
    totals = []
    for k in range(1, ny):
        copy = remote(
            total_row.at[y], total_row.at[y], total_send.at[k], total_recv.at[y],
            {"y": lax.rem(y + k, ny)},
        )
        copy.start()
        totals.append(copy)

    for h in range(heads):
        crow[h] = rows[h : h + 1]
    wide = heads * LANES
    pick2 = (iota((48, wide), 0) & 15) == lax.shift_right_logical(iota((48, wide), 1), 7)
    cum2[...] = dot(stacked, pick2.astype(BF16), ((0,), (0,)))
    gram[...] = dot(bcc[:, N : 2 * N], bcc[:, 0:N], ((1,), (1,)))
    left = iota((LANES, LANES), 1) < 64
    causal = iota((LANES, LANES), 0) >= iota((LANES, LANES), 1)
    loads[5].wait()

    def local_pair(i, _):
        lanes = pl.ds(pl.multiple_of(i * LANES, LANES), LANES)
        for block in range(length // LANES):
            t = slice(block * LANES, (block + 1) * LANES)
            results = []
            for side in range(2):
                h = 2 * i + side
                here = cum2[t, pl.ds(pl.multiple_of(h * LANES, LANES), LANES)]
                parts = []
                for other in range(block + 1):
                    s = slice(other * LANES, (other + 1) * LANES)
                    spread = here - crow[h, :, s]
                    if other == block:
                        part = jnp.where(causal, gram[t, s] * jnp.exp(jnp.minimum(spread, 0.0)), 0.0)
                    else:
                        part = gram[t, s] * jnp.exp(spread)
                    parts.append(part.astype(BF16))
                mixing = parts[0] if block == 0 else jnp.concatenate(parts, axis=1)
                results.append(dot(mixing, xc[0 : (block + 1) * LANES, lanes], ((1,), (0,))))
            skip = jnp.where(left, d_skip[2 * i], d_skip[2 * i + 1])
            ya[t, lanes] = jnp.where(left, results[0], results[1]) + skip * xc[t, lanes].astype(F32)
        return 0

    lax.fori_loop(0, 3, local_pair, 0)

    def y_copy(half, k):
        lanes = halves[half]
        return remote(
            y_buf.at[y, :, lanes], y_buf.at[y, :, lanes], y_send.at[half, k], y_recv.at[half, y],
            {"y": lax.rem(y + k, ny)},
        )

    for half, lanes in enumerate(halves):
        for k in row_steps:
            other = lax.rem(j + k, nj)
            theirs = row_buf.at[other, :, lanes]
            remote(
                theirs, theirs, row_send.at[half, k], row_recv.at[half, other], member(other)
            ).wait_recv()
        running = jnp.zeros((slab, lanes.stop - lanes.start), F32)
        for i in range(nj):
            prefix[i, :, lanes] = running
            running = jnp.exp(decay_row[i, :, lanes]) * running
            running = running + row_buf[i, :, lanes].astype(F32)
        y_buf[y, :, lanes] = running.astype(BF16)
        for k in y_steps:

            @pl.when(y + k < ny)
            def _(half=half, k=k):
                y_copy(half, k).start()

    n_blocks = length // ROWS
    pairs_first = jnp.where(y >= 3, pairs, 3)
    gates_first = jnp.where(y >= 3, n_blocks, 0)
    loads[6].wait()

    def gates(i, _):
        here = pl.ds(pl.multiple_of(i * ROWS, ROWS), ROWS)
        factor = silu(gate[here, :].astype(F32))
        ya[here, :] = ya[here, :] * factor
        yb[here, :] = jnp.exp(cum[here, :]) * factor
        return 0

    lax.fori_loop(3, pairs_first, local_pair, 0)
    lax.fori_loop(0, gates_first, gates, 0)

    for k in range(1, ny):
        other = lax.rem(y + k, ny)
        remote(
            total_row.at[other], total_row.at[other], total_send.at[k], total_recv.at[other],
            {"y": other},
        ).wait_recv()
    returned = []
    for half, lanes in enumerate(halves):
        for k in y_steps:

            @pl.when(y >= k)
            def _(half=half, lanes=lanes, k=k):
                other = lax.rem(y - k + ny, ny)
                theirs = y_buf.at[other, :, lanes]
                remote(
                    theirs, theirs, y_send.at[half, k], y_recv.at[half, other], {"y": other}
                ).wait_recv()

        def earlier(i, total, lanes=lanes):
            return jnp.exp(total_row[i, :, lanes]) * total + y_buf[i, :, lanes].astype(F32)

        part_width = lanes.stop - lanes.start
        base = lax.fori_loop(0, y, earlier, jnp.zeros((slab, part_width), F32))
        fade = jnp.zeros((1, part_width), F32)
        for i in range(nj):
            c_out[i, :, lanes] = (jnp.exp(fade) * base + prefix[i, :, lanes]).astype(BF16)
            fade = fade + decay_row[i, :, lanes]
        for k in row_steps:
            other = lax.rem(j + k, nj)
            copy = remote(
                c_out.at[other, :, lanes], carried.at[slice_of(j), lanes], c_send.at[half, k],
                c_recv.at[half, j], member(other),
            )
            copy.start()
            returned.append(copy)
        carried[slice_of(j), lanes] = c_out[j, :, lanes]

    lax.fori_loop(pairs_first, pairs, local_pair, 0)
    lax.fori_loop(gates_first, n_blocks, gates, 0)

    rows_out = out_ref.shape[0]
    sign = 1 - 2 * c
    n_long = nz // 2
    n_short = n_long - 1

    def towards(offset):
        return lax.rem(z + offset * sign + 2 * nz, nz)

    def turn(d):
        begin = lax.div(d * rows_out, LANES)

        def turn_block(i, _):
            here = pl.ds(pl.multiple_of((begin + i) * LANES, LANES), LANES)
            wt[here, :] = w[:, here].T
            return 0

        lax.fori_loop(0, pl.cdiv(rows_out, LANES), turn_block, 0)

    loads[8].wait()
    turn(towards(n_long))
    if n_short:
        turn(towards(-n_short))
    loads[7].wait()
    amount = gain[...].reshape(1, width)

    def await_carried(half):
        for k in row_steps:
            other = lax.rem(j + k, nj)
            theirs = carried.at[slice_of(other), halves[half]]
            remote(
                theirs, theirs, c_send.at[half, k], c_recv.at[half, other], member(other)
            ).wait_recv()

    def finish(half, here):
        lanes = halves[half]
        from_state = dot(bcc[here, N : 2 * N], carried[:, lanes], ((1,), (0,)))
        gated = ya[here, lanes] + yb[here, lanes] * from_state
        ut[lanes, here] = (gated * amount[:, lanes]).astype(BF16).T
        square = gated * gated
        total = square[:, 0:LANES]
        for begin in range(LANES, lanes.stop - lanes.start, LANES):
            total = total + square[:, begin : begin + LANES]
        sq_part[here, :] = total if half == 0 else sq_part[here, :] + total

    def finish_first(i, _):
        finish(0, pl.ds(pl.multiple_of(i * LANES, LANES), LANES))
        return 0

    await_carried(0)
    lax.fori_loop(0, length // LANES, finish_first, 0)

    piece = length // SUBS

    def tokens(q):
        return pl.ds(pl.multiple_of(q * piece, piece), piece)

    def project_piece(d, q):
        here = pl.ds(pl.multiple_of(d * rows_out, 64), rows_out)
        chunks[d, q] = dot(wt[here, :], ut[:, tokens(q)], ((1,), (0,))).astype(BF16)

    def project(d):
        here = pl.ds(pl.multiple_of(d * rows_out, 64), rows_out)
        part = dot(wt[here, :], ut[...], ((1,), (0,))).astype(BF16)
        for q in range(SUBS):
            chunks[d, q] = part[:, q * piece : (q + 1) * piece]

    def long_copy(source, step, q):
        return remote(
            source, long_in.at[step, q], long_send.at[step, q], long_recv.at[step, q],
            {"z": towards(1)},
        )

    def short_copy(source, step, q):
        return remote(
            source, short_in.at[step, q], short_send.at[step, q], short_recv.at[step, q],
            {"z": towards(-1)},
        )

    def begin(q, _):
        finish(1, tokens(q))
        project_piece(towards(n_long), q)
        long_copy(chunks.at[towards(n_long), q], 0, q).start()
        if n_short:
            project_piece(towards(-n_short), q)
            short_copy(chunks.at[towards(-n_short), q], 0, q).start()
        return 0

    await_carried(1)
    lax.fori_loop(0, SUBS, begin, 0)

    squares = jnp.zeros((16, length), F32)
    for term in split_three(sq_part[...]):
        squares = squares + dot(jnp.ones((16, LANES), BF16), term, ((1,), (1,)))
    sq_buf[z] = squares[0:1, :]
    shared = []
    for k in range(1, nz):
        copy = remote(
            sq_buf.at[z], sq_buf.at[z], sq_send.at[k], sq_recv.at[z], {"z": lax.rem(z + k, nz)}
        )
        copy.start()
        shared.append(copy)

    def turn_and_project(d):
        turn(d)
        project(d)

    if n_long == 1:
        turn_and_project(z)
    for step in range(1, n_long):
        turn_and_project(towards(n_long - step))
        if step < n_short:
            turn_and_project(towards(step - n_short))
        if step == n_long - 1:
            turn_and_project(z)

        def relay(q, _, step=step):
            long_copy(long_in.at[step - 1, q], step - 1, q).wait_recv()
            long_out[step - 1, q] = (
                long_in[step - 1, q].astype(F32) + chunks[towards(n_long - step), q].astype(F32)
            ).astype(BF16)
            long_copy(long_out.at[step - 1, q], step, q).start()
            if step < n_short:
                short_copy(short_in.at[step - 1, q], step - 1, q).wait_recv()
                short_out[step - 1, q] = (
                    short_in[step - 1, q].astype(F32)
                    + chunks[towards(step - n_short), q].astype(F32)
                ).astype(BF16)
                short_copy(short_out.at[step - 1, q], step, q).start()
            return 0

        lax.fori_loop(0, SUBS, relay, 0)

    for k in range(1, nz):
        other = lax.rem(z + k, nz)
        remote(sq_buf.at[other], sq_buf.at[other], sq_send.at[k], sq_recv.at[other], {"z": other}).wait_recv()
    def deliver(q, _):
        long_copy(long_in.at[n_long - 1, q], n_long - 1, q).wait_recv()
        total = chunks[z, q].astype(F32) + long_in[n_long - 1, q].astype(F32)
        if n_short:
            short_copy(short_in.at[n_short - 1, q], n_short - 1, q).wait_recv()
            total = total + short_in[n_short - 1, q].astype(F32)
        summed = sq_buf[0, :, tokens(q)]
        for i in range(1, nz):
            summed = summed + sq_buf[i, :, tokens(q)]
        scale = lax.rsqrt(summed * (1.0 / (width * nz)) + 1e-5)
        out_ref[:, tokens(q)] = (total * scale).astype(BF16)
        return 0

    lax.fori_loop(0, SUBS, deliver, 0)

    @pl.when(flat < ny * nj - 1)
    def _():
        for copy in halos:
            copy.wait_send()

    for copy in decays + totals + sent + returned + shared:
        copy.wait_send()
    for half in range(2):
        for k in y_steps:

            @pl.when(y + k < ny)
            def _(half=half, k=k):
                y_copy(half, k).wait_send()

    def drained(q, _):
        for step in range(n_long):
            long_copy(long_in.at[step, q], step, q).wait_send()
        for step in range(n_short):
            short_copy(short_in.at[step, q], step, q).wait_send()
        return 0

    lax.fori_loop(0, SUBS, drained, 0)


def shards(sizes, head_input, bc_input, conv_x, conv_bc, log_decay, d_skip, gate_z, norm_gain, w_out):
    ny, nx, nc, nz = sizes
    nj = nx * nc
    length, width = head_input.shape
    heads = log_decay.shape[0]
    slab = N // nj
    out_width = w_out.shape[1] // nz
    piece = length // SUBS
    n_long = nz // 2
    n_short = n_long - 1
    dma = pltpu.SemaphoreType.DMA
    vmem = pltpu.VMEM
    scratch = [
        vmem((length, width), BF16), vmem((length, 2 * N), BF16),
        vmem((K, width), F32), vmem((K, 2 * N), F32), vmem((heads, length), F32),
        pltpu.SMEM((heads,), F32), vmem((length, width), BF16), vmem((width,), F32),
        vmem(w_out.shape, BF16),
        dma((9,)),
        vmem((16, width), BF16), vmem((16, 2 * N), BF16), dma((2,)), dma((2,)),
        vmem((length, width), BF16), vmem((length, 2 * N), BF16),
        vmem((heads, 1, length), F32), vmem((length, width), F32), vmem((length, heads * LANES), F32),
        vmem((length, length), F32), vmem((length, width), BF16),
        vmem((N, width), F32), vmem((N, width), BF16),
        vmem((nj, 1, width), F32), dma((nj,)), dma((nj,)),
        vmem((ny, 1, width), F32), dma((ny,)), dma((ny,)),
        vmem((nj, slab, width), BF16), dma((2, nj)), dma((2, nj)), vmem((nj, slab, width), F32),
        vmem((ny, slab, width), BF16), dma((2, ny)), dma((2, ny)),
        vmem((nj, slab, width), BF16), vmem((N, width), BF16), dma((2, nj)), dma((2, nj)),
        vmem((length, width), F32), vmem((length, width), F32), vmem((length, LANES), F32),
        vmem((nz, 1, length), F32), dma((nz,)), dma((nz,)),
        vmem(w_out.shape[::-1], BF16), vmem((width, length), BF16),
        vmem((nz, SUBS, out_width, piece), BF16),
        vmem((max(n_long - 1, 1), SUBS, out_width, piece), BF16),
        vmem((max(n_short - 1, 1), SUBS, out_width, piece), BF16),
        vmem((n_long, SUBS, out_width, piece), BF16),
        vmem((max(n_short, 1), SUBS, out_width, piece), BF16),
        dma((n_long, SUBS)), dma((n_long, SUBS)),
        dma((max(n_short, 1), SUBS)), dma((max(n_short, 1), SUBS)),
    ]
    return pl.pallas_call(
        functools.partial(kernel, sizes),
        out_shape=pltpu.VMEM((out_width, length), BF16),
        in_specs=[pl.BlockSpec(memory_space=pl.ANY)] * 9,
        out_specs=pl.BlockSpec(memory_space=pltpu.VMEM),
        scratch_shapes=scratch,
        compiler_params=pltpu.CompilerParams(
            collective_id=0, has_side_effects=True, vmem_limit_bytes=60 * 1024 * 1024
        ),
        name="layer",
    )(
        head_input, bc_input, conv_x, conv_bc, log_decay, d_skip, gate_z,
        norm_gain, w_out,
    ).T


def solution(mesh):
    n_ctx, nz = mesh.devices.shape
    sizes = (8, 4, 2, nz) if n_ctx == 64 else (2, max(n_ctx // 4, 1), 2, nz)
    split = Mesh(mesh.devices.reshape(sizes), ("y", "x", "c", "z"))
    return jax.shard_map(
        functools.partial(shards, sizes),
        mesh=split,
        in_specs=(
            P(CTX, "z"), P(CTX, None), P(None, "z"), P(), P("z", CTX), P("z"), P(CTX, "z"),
            P("z"), P("z", None),
        ),
        out_specs=P(CTX, "z"),
        check_vma=False,
    )
```
